256 devices in a mesh: group: 8 (over x_lo, y), member: 32 (over x_hi, z, core).
Axes of the slice: x: 4 (x_hi: 2, x_lo: 2; x = x_hi * 2 + x_lo), y: 4, z: 8, core: 2. Of those that a mesh axis runs over, the one named last changes fastest.
Arguments:
- entity: bfloat16 [65536, 800], P(('group', 'member')), may hold values from -3 to 7.5
- adagrad_state: float32 [65536], P(('group', 'member')), may hold values from 0.01 to 1
- relation: bfloat16 [1345, 800], replicated, may hold values from -1.8 to 1.8
- source_ids: int32 [2, 131072], P(None, ('group', 'member')), may hold values from 0 to 255
- relation_ids: int32 [2, 131072], P(None, ('group', 'member')), may hold values from 0 to 1344
- dest_groups: int32 [2, 131072, 1], P(None, ('group', 'member')), may hold values from 0 to 7; in each aligned block of 512 rows (0 to 511, 512 to 1023, ..., all dimensions but the last counted through in order) at most 128 rows name the same one
- dest_rows: int32 [2, 131072], P(None, ('group', 'member')), may hold values from 0 to 255
- negative_ids: int32 [2, 256000], P(None, ('group', 'member')), may hold values from 0 to 255
- owners: int32 [2, 8], replicated, may hold values from 0 to 31
Outputs:
- new_entity: bfloat16 [65536, 800], P(('group', 'member'))
- new_state: float32 [65536], P(('group', 'member'))
The draws below stay inside these ranges and needn't reach their ends.
Inputs may be any that keep to these rules, and one draw needn't show every extreme that they name: `dest_groups`: for each sub-step and each device's 512 edges, at most 128 name any one destination group, a bound that some block reaches.
All inputs are finite; a program needn't handle non-finite values.
Results may differ from the reference program's by a relative error of at most 0.017.
Values may be sent and summed in bfloat16 or wider, within the bound.
A program may use at most 64 MiB of HBM per device.

```python
import math
import jax
import jax.numpy as jnp
import numpy as np
from jax import lax

DIM = 400
REL = 1345
NEG = 1000
SUBSTEPS = 2
ROWS_DEV = 256
EDGES = 512
CAP = 128
ENTITIES = 65536
EDGES_ALL = 131072
NEG_ALL = 256000
N_GROUP = 8
N_MEMBER = 32


def draw_entity(key, part):
    first = jax.random.fold_in(key, 0)
    values = jnp.clip(jax.random.normal(first, (ENTITIES, 2 * DIM), jnp.float32), -6.0, 6.0)
    out = values * 0.5
    return out.astype(jnp.bfloat16)


def draw_relation(key, part):
    first = jax.random.fold_in(key, 0)
    values = jnp.clip(jax.random.normal(first, (REL, 2 * DIM), jnp.float32), -6.0, 6.0)
    out = values * 0.3
    return out.astype(jnp.bfloat16)


def place_ends(array, rng, low, high):
    index_at = [jax.random.randint(jax.random.fold_in(rng, axis), (), 0, length) for axis, length in enumerate(array.shape)]
    widest = array.shape.index(max(array.shape))
    beside = index_at[:widest] + [(index_at[widest] + 1) % array.shape[widest]] + index_at[widest + 1:]
    return array.at[tuple(index_at)].set(low).at[tuple(beside)].set(high)


def levels(key, shape, shards, smallest, largest):
    loudness, own = 1.0, jax.random.fold_in(key, 6)
    for dim, parts in shards:
        draws = jnp.exp(jax.random.uniform(jax.random.fold_in(own, dim), (parts,), jnp.float32, smallest / len(shards), largest / len(shards)))
        loudness = loudness * jnp.repeat(draws, shape[dim] // parts).reshape([-1 if axis == dim else 1 for axis in range(len(shape))])
    return loudness


def cumulative_ranks(number_of, slope):
    loads = [(1 << 20) // math.isqrt(grade ** slope) + 1 for grade in range(1, number_of + 1)]
    spread = 1 + sum(loads) // (1 << 30)
    return np.cumsum(np.array([max(1, weight // spread) for weight in loads]))


def skewed_ids(stream_key, extent, number_of, lean):
    table = cumulative_ranks(number_of, lean)
    lot = jax.random.randint(jax.random.fold_in(stream_key, 1), extent, 0, int(table[number_of - 1]))
    standing = jnp.searchsorted(jnp.asarray(table, jnp.int32), lot, side="right")
    return jax.random.permutation(jax.random.fold_in(stream_key, 2), number_of)[standing].astype(jnp.int32)


def routed_block(rng, own, number, rows, number_of, top, most, lean):
    order = jax.random.permutation(rng, number_of)
    heavy_load, usual = portions_of(number_of, rows * top, most, lean, True), portions_of(number_of, rows * top, most, lean, False)
    places = jnp.arange(number_of)

    def named(tallies, turn):
        used = int((tallies > 0).sum())
        fixed = max(1, used // 4)
        moved = fixed + (places - fixed + turn * (used - fixed)) % max(1, number_of - fixed)
        return jnp.zeros((number_of,), jnp.int32).at[order[jnp.where(places < fixed, places, moved)]].set(jnp.asarray(tallies, jnp.int32))

    tallies = jnp.where(number % 4 == 0, named(heavy_load, number // 4), named(usual, number - number // 4 - 1))
    mixed = jax.random.permutation(jax.random.fold_in(own, 3), number_of)
    donor, sink = mixed[0:number_of // 2 * 2:2], mixed[1:number_of // 2 * 2:2]
    slack = jnp.minimum(tallies[donor] - 1, most - tallies[sink]) // 2
    slack = jnp.where((donor == order[0]) | (sink == order[0]) | (tallies[sink] == 0), 0, jnp.maximum(slack, 0))
    moved = jax.random.randint(jax.random.fold_in(own, 4), (number_of // 2,), 0, 1 << 20) % (slack + 1)
    tallies = tallies.at[donor].add(-moved).at[sink].add(moved)
    items = jnp.searchsorted(jnp.cumsum(tallies), jnp.arange(rows * top), side="right").astype(jnp.int32)
    grid = items.reshape(top, rows).T
    grid = grid[jax.random.permutation(jax.random.fold_in(own, 1), rows)]
    turn = jax.random.randint(jax.random.fold_in(own, 2), (rows, 1), 0, top)
    return jnp.take_along_axis(grid, (jnp.arange(top)[None, :] + turn) % top, axis=1)


def portions_of(number_of, total, bound, lean, full):
    loads = [(1 << 20) // math.isqrt(grade ** lean) + 1 for grade in range(1, number_of + 1)]
    largest = bound if full else min(bound, max(-(-total // number_of), total * loads[0] // sum(loads)))
    least = 1 if total - largest >= number_of - 1 else 0
    given, spare = [largest] + [least] * (number_of - 1), total - largest - least * (number_of - 1)
    while spare > 0:
        free = [i for i in range(1, number_of) if given[i] < largest] or [i for i in range(1, number_of) if given[i] < bound]
        whole, remaining = sum([loads[i] for i in free]), spare
        for i in free:
            extra = min(bound - given[i], max(1, remaining * loads[i] // whole), spare)
            given[i] = given[i] + extra
            spare = spare - extra
    return np.array(given)


def setup_inputs(seed: int = 0) -> dict:
    arg_keys = jax.random.split(jax.random.key(seed), 10)
    entity = draw_entity(jax.random.fold_in(arg_keys[9], 71), 0)
    adagrad_state = jnp.clip(jnp.exp(math.log(1.0) - 4.6051702 * jax.random.uniform(arg_keys[1], (ENTITIES,), jnp.float32) ** levels(arg_keys[1], (ENTITIES,), ((0, 256),), -0.2, 0.2)), 0.01, 1.0)
    relation = draw_relation(jax.random.fold_in(arg_keys[9], 71), 0)
    source_ids = place_ends(jax.random.randint(arg_keys[3], (SUBSTEPS, EDGES_ALL), 0, ROWS_DEV), jax.random.fold_in(arg_keys[3], 1), 0, ROWS_DEV - 1).astype(jnp.int32)
    relation_ids = place_ends(skewed_ids(arg_keys[4], (SUBSTEPS, EDGES_ALL), REL, 2), jax.random.fold_in(arg_keys[4], 3), 0, REL - 1).astype(jnp.int32)
    dest_groups_keys = jax.random.split(jax.random.fold_in(arg_keys[5], 1), SUBSTEPS * EDGES_ALL // EDGES)
    dest_groups_turns = jax.random.permutation(jax.random.fold_in(arg_keys[5], 3), SUBSTEPS * EDGES_ALL // EDGES)
    dest_groups = jax.vmap(lambda own, number: routed_block(jax.random.fold_in(arg_keys[5], 2), own, number, EDGES, N_GROUP, 1, CAP, 2))(dest_groups_keys, dest_groups_turns).reshape((SUBSTEPS, EDGES_ALL, 1))
    dest_rows = place_ends(jax.random.randint(arg_keys[6], (SUBSTEPS, EDGES_ALL), 0, ROWS_DEV), jax.random.fold_in(arg_keys[6], 1), 0, ROWS_DEV - 1).astype(jnp.int32)
    negative_ids = place_ends(jax.random.randint(arg_keys[7], (SUBSTEPS, NEG_ALL), 0, ROWS_DEV), jax.random.fold_in(arg_keys[7], 1), 0, ROWS_DEV - 1).astype(jnp.int32)
    owners = place_ends(jax.random.randint(arg_keys[8], (SUBSTEPS, N_GROUP), 0, N_MEMBER), jax.random.fold_in(arg_keys[8], 1), 0, N_MEMBER - 1).astype(jnp.int32)
    return dict(entity=entity, adagrad_state=adagrad_state, relation=relation, source_ids=source_ids, relation_ids=relation_ids, dest_groups=dest_groups, dest_rows=dest_rows, negative_ids=negative_ids, owners=owners)


def complex_query(source, rel):
    half = source.shape[-1] // 2
    sr, si = (source[..., :half], source[..., half:])
    rr, ri = (rel[..., :half], rel[..., half:])
    return jnp.concatenate([sr * rr - si * ri, sr * ri + si * rr], -1)

def source_grad(grad_query, rel):
    half = grad_query.shape[-1] // 2
    gr, gi = (grad_query[..., :half], grad_query[..., half:])
    rr, ri = (rel[..., :half], rel[..., half:])
    return jnp.concatenate([gr * rr + gi * ri, gi * rr - gr * ri], -1)

def edge_terms(source_rows, rel_rows, dest_rows, negatives):
    rel = rel_rows.astype(jnp.float32)
    query = complex_query(source_rows.astype(jnp.float32), rel).astype(jnp.bfloat16)
    dest = dest_rows.astype(jnp.float32)
    positive = lax.optimization_barrier(jnp.sum(query.astype(jnp.float32) * dest, -1))
    scores = lax.dot_general(query, negatives, (((1,), (1,)), ((), ())), preferred_element_type=jnp.float32)
    top = jnp.maximum(lax.optimization_barrier(jnp.max(scores, 1)), positive)
    pos_exp = jnp.exp(positive - top)
    neg_exp = jnp.exp(scores - top[:, None])
    total = pos_exp + lax.optimization_barrier(jnp.sum(neg_exp, 1))
    coef_pos = pos_exp / total - 1.0
    coef_neg = (neg_exp / total[:, None]).astype(jnp.bfloat16)
    grad_query = coef_pos[:, None] * dest + jnp.dot(coef_neg, negatives, preferred_element_type=jnp.float32)
    grad_source = source_grad(grad_query, rel)
    grad_dest = coef_pos[:, None] * query.astype(jnp.float32)
    grad_neg = lax.dot_general(coef_neg, query, (((0,), (0,)), ((), ())), preferred_element_type=jnp.float32)
    return (grad_source, grad_dest, grad_neg)

def reference(entity, adagrad_state, relation, source_ids, relation_ids, dest_groups, dest_rows, negative_ids, owners):
    members = N_MEMBER
    count = N_GROUP * N_MEMBER
    width = entity.shape[1]
    table = entity.reshape(count, ROWS_DEV, width)
    state = adagrad_state.reshape(count, ROWS_DEV)
    for step in range(SUBSTEPS):
        src = source_ids[step].reshape(count, EDGES)
        rel = relation_ids[step].reshape(count, EDGES)
        dgr = dest_groups[step, :, 0].reshape(count, EDGES)
        drw = dest_rows[step].reshape(count, EDGES)
        neg = negative_ids[step].reshape(count, NEG)
        own = owners[step]

        def visit(total, device):
            grp = device // members
            mem = device % members
            owner_dev = (grp * members + own[grp]).astype(jnp.int32)
            block = table[owner_dev]
            dest_dev = (dgr[device] * members + mem).astype(jnp.int32)
            source_rows = block[src[device]]
            rel_rows = relation[rel[device]]
            dest_vals = table[dest_dev, drw[device]]
            negatives = table[device][neg[device]]
            grad_source, grad_dest, grad_neg = edge_terms(source_rows, rel_rows, dest_vals, negatives)
            total = total.at[owner_dev, src[device]].add(grad_source)
            total = total.at[dest_dev, drw[device]].add(grad_dest)
            total = total.at[device, neg[device]].add(grad_neg)
            return (total, None)
        grads, _ = lax.scan(visit, jnp.zeros((count, ROWS_DEV, width), jnp.float32), jnp.arange(count, dtype=jnp.int32))
        state = state + lax.optimization_barrier(jnp.mean(grads * grads, -1))
        table = (table.astype(jnp.float32) - 1.0 * grads / jnp.sqrt(state)[..., None]).astype(jnp.bfloat16)
    return (table.reshape(count * ROWS_DEV, width), state.reshape(count * ROWS_DEV))
```

```python
import functools

import jax
import jax.numpy as jnp
from jax import lax
from jax.experimental import pallas as pl
from jax.experimental.pallas import tpu as pltpu
from jax.sharding import PartitionSpec as P

MESH = pl.DeviceIdType.MESH
F32 = jnp.float32
BF16 = jnp.bfloat16
LANES = 128
CAP = 128
LOW = -1e30


def dot_nn(a, b):
    return lax.dot_general(a, b, (((1,), (0,)), ((), ())), preferred_element_type=F32)


def dot_nt(a, b):
    return lax.dot_general(a, b, (((1,), (1,)), ((), ())), preferred_element_type=F32)


def dot_tn(a, b):
    return lax.dot_general(a, b, (((0,), (0,)), ((), ())), preferred_element_type=F32)


def iota(shape, dim):
    return lax.broadcasted_iota(jnp.int32, shape, dim)


def onehot(mask):
    return jnp.where(mask, 1.0, 0.0).astype(BF16)


def complex_parts(value, main):
    return value[:, :main], value[:, main : 2 * main], value[:, 2 * main :]


def tail_forms(tail, first):
    swapped = pltpu.roll(tail, LANES // 2, 1)
    return jnp.where(first, tail, swapped), jnp.where(first, swapped, tail)


def times(source, rel, main, first, sign):
    sr, si, st = complex_parts(source, main)
    rr, ri, rt = complex_parts(rel, main)
    tr, ti = tail_forms(rt, first)
    mixed = st * tr + sign * (pltpu.roll(st, LANES // 2, 1) * ti)
    return jnp.concatenate([sr * rr - si * ri, sr * ri + si * rr, mixed], 1)


def times_conjugate(grad, rel, main, first, sign):
    gr, gi, gt = complex_parts(grad, main)
    rr, ri, rt = complex_parts(rel, main)
    tr, ti = tail_forms(rt, first)
    mixed = gt * tr - sign * (pltpu.roll(gt, LANES // 2, 1) * ti)
    return jnp.concatenate([gr * rr + gi * ri, gi * rr - gr * ri, mixed], 1)


def kernel(
    groups,
    members,
    owners,
    entity,
    state_in,
    relation,
    source_ids,
    relation_ids,
    dest_groups,
    dest_rows,
    negative_ids,
    entity_out,
    state_out,
    place,
    table,
    state,
    rel_table,
    slot_src,
    slot_rel,
    src_rows,
    ids_send,
    ids_recv,
    counts,
    rel_slots,
    query,
    neg_exp,
    neg_max,
    neg_sum,
    weights,
    row_send,
    row_recv,
    grad_send,
    grad_recv,
    source_acc,
    grads,
    ar_in,
    ar_half,
    ar_mine,
    ar_parts,
    ar_piece,
    ar_other,
    ar_out,
    ids_ss,
    ids_rs,
    row_ss,
    row_rs,
    grad_ss,
    grad_rs,
    p1_ss,
    p1_rs,
    p2_ss,
    p2_rs,
    p3_ss,
    p3_rs,
    p4_ss,
    p4_rs,
    p5_ss,
    p5_rs,
):
    steps, edges = source_ids.shape
    rows, width = entity.shape
    rel_rows = relation.shape[0]
    half = width // 2
    main = half // LANES * LANES
    wide = table.shape[1]
    slots = groups * CAP
    depth = members // 4
    rings = groups // 2

    g = lax.axis_index("group")
    m = lax.axis_index("member")
    gx, gy = g // rings, g % rings
    core, z, xh = m % 2, (m // 2) % depth, m // (2 * depth)
    twin = m + 1 - 2 * core
    across = (m + 2 * depth) % members

    def peer(k):
        return ((gx + k // rings) % 2) * rings + (gy + k % rings) % rings

    def floor(k):
        return (z + k) % depth

    def along(other):
        return (g, xh * (2 * depth) + other * 2 + core)

    def remote(src, dst, send_sem, recv_sem, device):
        return pltpu.make_async_remote_copy(
            src_ref=src,
            dst_ref=dst,
            send_sem=send_sem,
            recv_sem=recv_sem,
            device_id=device,
            device_id_type=MESH,
        )

    barrier = pltpu.get_barrier_semaphore()

    @pl.loop(1, groups)
    def _(k):
        pl.semaphore_signal(barrier, inc=1, device_id=(peer(k), m), device_id_type=MESH)

    @pl.loop(1, depth)
    def _(k):
        pl.semaphore_signal(barrier, inc=1, device_id=along(floor(k)), device_id_type=MESH)

    pl.semaphore_signal(barrier, inc=1, device_id=(g, twin), device_id_type=MESH)
    pl.semaphore_signal(barrier, inc=1, device_id=(g, across), device_id_type=MESH)

    comp = iota((width, 1), 0)
    imag = comp >= half
    local = jnp.where(imag, comp - half, comp)
    spot = jnp.where(
        local < main,
        local + jnp.where(imag, main, 0),
        2 * main + jnp.where(imag, LANES // 2, 0) + local - main,
    )
    place[...] = onehot(iota((width, wide), 1) == spot)
    table[...] = dot_nn(entity[...], place[...]).astype(BF16)
    eye = iota((rows, rows), 0) == iota((rows, rows), 1)
    state[...] = jnp.sum(jnp.where(eye, state_in[...], 0.0), 1, keepdims=True)

    ids_send[...] = jnp.zeros_like(ids_send)
    for s in range(steps):
        group_row = dest_groups[s : s + 1, :]
        named = iota((16, edges), 0) == group_row
        before = onehot(iota((edges, edges), 0) < iota((edges, edges), 1))
        rank = dot_nn(onehot(named), before)
        rank = jnp.sum(jnp.where(named, rank, 0.0), 0, keepdims=True)
        slot_row = group_row * CAP + rank.astype(jnp.int32)
        taken = onehot(iota((slots, edges), 0) == slot_row)
        rel_row = relation_ids[s : s + 1, :]
        high = rel_row // 32
        which = iota((16, edges), 0)
        facts = jnp.where(which == 0, source_ids[s : s + 1, :], 0)
        facts = jnp.where(which == 1, high, facts)
        facts = jnp.where(which == 2, rel_row - 32 * high, facts)
        facts = jnp.where(which == 3, dest_rows[s : s + 1, :], facts)
        facts = jnp.where(which == 4, 1, facts)
        facts = facts.astype(F32).astype(BF16)
        flat = dot_nt(facts, taken).astype(jnp.int32)
        tall = dot_nt(taken, facts).astype(jnp.int32)
        empty_flat = flat[4:5, :] - 1
        empty_tall = tall[:, 4:5] - 1
        src_rows[s] = flat[0:1, :] + 4 * rows * empty_flat
        slot_src[s] = tall[:, 0:1] + 4 * rows * empty_tall
        slot_rel[s] = 32 * tall[:, 1:2] + tall[:, 2:3] + 4 * rel_rows * empty_tall
        wanted = flat[3:4, :] + 4 * rows * empty_flat
        for d in range(groups):
            ids_send[d, s : s + 1, :] = wanted[:, d * CAP : (d + 1) * CAP]

    pl.semaphore_wait(barrier, groups + depth)

    def ids_copy(d):
        return remote(ids_send.at[d], ids_recv.at[g], ids_ss.at[d], ids_rs.at[g], (d, m))

    def ids_arrival(d):
        return remote(ids_send.at[d], ids_recv.at[d], ids_ss.at[d], ids_rs.at[d], (d, m))

    @pl.loop(1, groups)
    def _(k):
        ids_copy(peer(k)).start()

    ids_recv[g] = ids_send[g]
    rel_table[...] = dot_nn(relation[...], place[...]).astype(BF16)

    @pl.loop(1, groups)
    def _(k):
        d = peer(k)
        ids_copy(d).wait_send()
        ids_arrival(d).wait_recv()

    first = iota((1, LANES), 1) < LANES // 2
    sign = jnp.where(first, -1.0, 1.0)

    def ar_start(i):
        remote(
            ar_in.at[i, 1 - core], ar_half.at[i], p1_ss.at[i], p1_rs.at[i], (g, twin)
        ).start()

    def ar_scatter_copy(i, other):
        return remote(
            ar_mine.at[i, other],
            ar_parts.at[i, z],
            p2_ss.at[i, other],
            p2_rs.at[i, z],
            along(other),
        )

    def ar_scatter_arrival(i, other):
        return remote(
            ar_mine.at[i, other],
            ar_parts.at[i, other],
            p2_ss.at[i, other],
            p2_rs.at[i, other],
            along(other),
        )

    def ar_gather_copy(i, other):
        return remote(
            ar_out.at[i, core, z],
            ar_out.at[i, core, z],
            p4_ss.at[i, other],
            p4_rs.at[i, z],
            along(other),
        )

    def ar_gather_arrival(i, other):
        return remote(
            ar_out.at[i, core, other],
            ar_out.at[i, core, other],
            p4_ss.at[i, other],
            p4_rs.at[i, other],
            along(other),
        )

    def ar_scatter(i):
        remote(
            ar_in.at[i, 1 - core], ar_half.at[i], p1_ss.at[i], p1_rs.at[i], (g, twin)
        ).wait()
        mine = ar_in[i, core].astype(F32) + ar_half[i].astype(F32)
        ar_mine[i] = mine.astype(BF16).reshape(depth, rows // 2 // depth, wide)

        @pl.loop(1, depth)
        def _(k):
            ar_scatter_copy(i, floor(k)).start()

    def ar_cross(i):
        @pl.loop(1, depth)
        def _(k):
            other = floor(k)
            ar_scatter_copy(i, other).wait_send()
            ar_scatter_arrival(i, other).wait_recv()

        ar_parts[i, z] = ar_mine[i, z]
        piece = jnp.sum(ar_parts[i].astype(F32), 0)
        ar_piece[i] = piece.astype(BF16)
        copy = remote(ar_piece.at[i], ar_other.at[i], p3_ss.at[i], p3_rs.at[i], (g, across))
        copy.start()
        copy.wait()
        whole = ar_piece[i].astype(F32) + ar_other[i].astype(F32)
        ar_out[i, core, z] = whole.astype(BF16)

        @pl.loop(1, depth)
        def _(k):
            ar_gather_copy(i, floor(k)).start()

    def ar_finish(i):
        @pl.loop(1, depth)
        def _(k):
            other = floor(k)
            ar_gather_copy(i, other).wait_send()
            ar_gather_arrival(i, other).wait_recv()

        out = remote(
            ar_out.at[i, core], ar_out.at[i, core], p5_ss.at[i], p5_rs.at[i], (g, twin)
        )
        back = remote(
            ar_out.at[i, 1 - core], ar_out.at[i, 1 - core], p5_ss.at[i], p5_rs.at[i], (g, twin)
        )
        out.start()
        out.wait_send()
        back.wait_recv()

    @pl.loop(0, steps)
    def _(s):
        root = owners[s, g]
        fetch, reduce = 2 * s, 2 * s + 1
        kept = jnp.where(m == root, table[...].astype(F32), 0.0).astype(BF16)
        ar_in[fetch] = kept.reshape(2, rows // 2, wide)
        ar_start(fetch)

        def row_copy(d):
            return remote(
                row_send.at[s, d], row_recv.at[s, g], row_ss.at[s, d], row_rs.at[s, g], (d, m)
            )

        def row_arrival(d):
            return remote(
                row_send.at[s, d], row_recv.at[s, d], row_ss.at[s, d], row_rs.at[s, d], (d, m)
            )

        def grad_copy(d):
            return remote(
                grad_send.at[s, d], grad_recv.at[s, g], grad_ss.at[s, d], grad_rs.at[s, g], (d, m)
            )

        def grad_arrival(d):
            return remote(
                grad_send.at[s, d], grad_recv.at[s, d], grad_ss.at[s, d], grad_rs.at[s, d], (d, m)
            )

        def asked(d):
            return onehot(iota((rows, CAP), 0) == ids_recv[d, pl.ds(s, 1), :])

        @pl.loop(1, groups)
        def _(k):
            d = peer(k)
            row_send[s, d] = dot_tn(asked(d), table[...]).astype(BF16)
            row_copy(d).start()

        row_recv[s, g] = dot_tn(asked(g), table[...]).astype(BF16)
        ar_scatter(fetch)

        slot_count = negative_ids.shape[1]
        hits = onehot(iota((rows, slot_count), 0) == negative_ids[pl.ds(s, 1), :])
        counts[...] = dot_nt(jnp.ones((8, slot_count), BF16), hits)

        def relations(k):
            base = pl.multiple_of(k * 2 * CAP, 2 * CAP)
            chosen = onehot(iota((2 * CAP, rel_rows), 1) == slot_rel[s, pl.ds(base, 2 * CAP), :])
            rel_slots[pl.ds(base, 2 * CAP), :] = dot_nn(chosen, rel_table[...]).astype(BF16)

        @pl.loop(0, groups // 4)
        def _(k):
            relations(k)

        ar_cross(fetch)

        @pl.loop(groups // 4, groups // 2)
        def _(k):
            relations(k)

        ar_finish(fetch)

        count_row = counts[0:1, :]
        present = count_row > 0.5

        @pl.loop(0, groups)
        def _(d):
            base = pl.multiple_of(d * CAP, CAP)
            here = pl.ds(base, CAP)
            chosen = onehot(iota((CAP, rows), 1) == slot_src[s, here, :])
            source = dot_nn(chosen, ar_out[fetch].reshape(rows, wide))
            q = times(source, rel_slots[here, :].astype(F32), main, first, sign).astype(BF16)
            query[here, :] = q
            scores = jnp.where(present, dot_nt(q, table[...]), LOW)
            top = jnp.max(scores, 1, keepdims=True)
            e = jnp.exp(scores - top) * count_row
            neg_exp[here, :] = e
            neg_max[here, :] = top
            neg_sum[here, :] = jnp.sum(e, 1, keepdims=True)

        source_acc[...] = jnp.zeros_like(source_acc)

        @pl.loop(0, groups)
        def _(k):
            d = peer(k)

            @pl.when(k > 0)
            def _():
                row_copy(d).wait_send()
                row_arrival(d).wait_recv()

            base = pl.multiple_of(d * CAP, CAP)
            here = pl.ds(base, CAP)
            q = query[here, :].astype(F32)
            dest = row_recv[s, d].astype(F32)
            positive = jnp.sum(q * dest, 1, keepdims=True)
            low = neg_max[here, :]
            top = jnp.maximum(low, positive)
            pos_exp = jnp.exp(positive - top)
            shrink = jnp.exp(low - top)
            total = pos_exp + neg_sum[here, :] * shrink
            coef_pos = pos_exp / total - 1.0
            grad_send[s, d] = (coef_pos * q).astype(BF16)

            @pl.when(k > 0)
            def _():
                grad_copy(d).start()

            coef_neg = (neg_exp[here, :] * (shrink / total)).astype(BF16)
            weights[here, :] = coef_neg
            grad_query = coef_pos * dest + dot_nn(coef_neg, table[...])
            grad_source = times_conjugate(
                grad_query, rel_slots[here, :].astype(F32), main, first, sign
            ).astype(BF16)
            spread = onehot(iota((rows, CAP), 0) == src_rows[s, :, here])
            source_acc[...] += dot_nn(spread, grad_source)

        ar_in[reduce] = source_acc[...].astype(BF16).reshape(2, rows // 2, wide)
        ar_start(reduce)
        grad_recv[s, g] = grad_send[s, g]
        ar_scatter(reduce)
        grads[...] = dot_tn(weights[...], query[...])
        ar_cross(reduce)
        ar_finish(reduce)

        @pl.loop(1, groups)
        def _(k):
            d = peer(k)
            grad_copy(d).wait_send()
            grad_arrival(d).wait_recv()

        @pl.loop(0, groups)
        def _(d):
            grads[...] += dot_nn(asked(d), grad_recv[s, d])

        total = grads[...] + jnp.where(
            m == root, ar_out[reduce].reshape(rows, wide).astype(F32), 0.0
        )
        fresh = state[...] + jnp.sum(total * total, 1, keepdims=True) * (1.0 / width)
        state[...] = fresh
        table[...] = (table[...].astype(F32) - total / jnp.sqrt(fresh)).astype(BF16)

    entity_out[...] = dot_nt(table[...], place[...]).astype(BF16)
    state_out[...] = jnp.sum(jnp.where(eye, state[...], 0.0), 0, keepdims=True)


def per_device(
    groups,
    members,
    entity,
    adagrad_state,
    relation,
    source_ids,
    relation_ids,
    dest_groups,
    dest_rows,
    negative_ids,
    owners,
):
    rows, width = entity.shape
    steps, edges = source_ids.shape
    half = width // 2
    wide = 2 * (half // LANES * LANES) + LANES
    slots = groups * CAP
    depth = members // 4
    piece = rows // 2 // depth
    uses = 2 * steps
    dma = pltpu.SemaphoreType.DMA
    vmem = pltpu.VMEM
    whole = pl.BlockSpec(memory_space=pltpu.VMEM)
    table, state = pl.pallas_call(
        functools.partial(kernel, groups, members),
        out_shape=(
            jax.ShapeDtypeStruct((rows, width), BF16),
            jax.ShapeDtypeStruct((1, rows), F32),
        ),
        in_specs=[pl.BlockSpec(memory_space=pltpu.SMEM)] + [whole] * 8,
        out_specs=(whole, whole),
        scratch_shapes=[
            vmem((width, wide), BF16),
            vmem((rows, wide), BF16),
            vmem((rows, 1), F32),
            vmem((relation.shape[0], wide), BF16),
            vmem((steps, slots, 1), jnp.int32),
            vmem((steps, slots, 1), jnp.int32),
            vmem((steps, 1, slots), jnp.int32),
            vmem((groups, 8, CAP), jnp.int32),
            vmem((groups, 8, CAP), jnp.int32),
            vmem((8, rows), F32),
            vmem((slots, wide), BF16),
            vmem((slots, wide), BF16),
            vmem((slots, rows), F32),
            vmem((slots, 1), F32),
            vmem((slots, 1), F32),
            vmem((slots, rows), BF16),
            vmem((steps, groups, CAP, wide), BF16),
            vmem((steps, groups, CAP, wide), BF16),
            vmem((steps, groups, CAP, wide), BF16),
            vmem((steps, groups, CAP, wide), BF16),
            vmem((rows, wide), F32),
            vmem((rows, wide), F32),
            vmem((uses, 2, rows // 2, wide), BF16),
            vmem((uses, rows // 2, wide), BF16),
            vmem((uses, depth, piece, wide), BF16),
            vmem((uses, depth, piece, wide), BF16),
            vmem((uses, piece, wide), BF16),
            vmem((uses, piece, wide), BF16),
            vmem((uses, 2, depth, piece, wide), BF16),
            dma((groups,)),
            dma((groups,)),
            dma((steps, groups)),
            dma((steps, groups)),
            dma((steps, groups)),
            dma((steps, groups)),
            dma((uses,)),
            dma((uses,)),
            dma((uses, depth)),
            dma((uses, depth)),
            dma((uses,)),
            dma((uses,)),
            dma((uses, depth)),
            dma((uses, depth)),
            dma((uses,)),
            dma((uses,)),
        ],
        compiler_params=pltpu.CompilerParams(
            collective_id=0, has_side_effects=True, vmem_limit_bytes=60 << 20
        ),
    )(
        owners,
        entity,
        adagrad_state.reshape(1, rows),
        relation,
        source_ids,
        relation_ids,
        dest_groups.reshape(steps, edges),
        dest_rows,
        negative_ids,
    )
    return (table, state.reshape(rows))


def solution(mesh):
    placed = (
        P(("group", "member"), None),
        P(("group", "member")),
        P(),
        P(None, ("group", "member")),
        P(None, ("group", "member")),
        P(None, ("group", "member"), None),
        P(None, ("group", "member")),
        P(None, ("group", "member")),
        P(),
    )
    return jax.shard_map(
        functools.partial(per_device, mesh.shape["group"], mesh.shape["member"]),
        mesh=mesh,
        in_specs=placed,
        out_specs=(P(("group", "member"), None), P(("group", "member"))),
        check_vma=False,
    )
```

```python
import functools

import jax
import jax.numpy as jnp
from jax import lax
from jax.experimental import pallas as pl
from jax.experimental.pallas import tpu as pltpu
from jax.sharding import PartitionSpec as P

MESH = pl.DeviceIdType.MESH
F32 = jnp.float32
BF16 = jnp.bfloat16
LANES = 128
CAP = 128
LOW = -1e30


def dot_nn(a, b):
    return lax.dot_general(a, b, (((1,), (0,)), ((), ())), preferred_element_type=F32)


def dot_nt(a, b):
    return lax.dot_general(a, b, (((1,), (1,)), ((), ())), preferred_element_type=F32)


def dot_tn(a, b):
    return lax.dot_general(a, b, (((0,), (0,)), ((), ())), preferred_element_type=F32)


def iota(shape, dim):
    return lax.broadcasted_iota(jnp.int32, shape, dim)


def onehot(mask):
    return jnp.where(mask, 1.0, 0.0).astype(BF16)


def complex_parts(value, main):
    return value[:, :main], value[:, main : 2 * main], value[:, 2 * main :]


def tail_forms(tail, first):
    swapped = pltpu.roll(tail, LANES // 2, 1)
    return jnp.where(first, tail, swapped), jnp.where(first, swapped, tail)


def times(source, rel, main, first, sign):
    sr, si, st = complex_parts(source, main)
    rr, ri, rt = complex_parts(rel, main)
    tr, ti = tail_forms(rt, first)
    mixed = st * tr + sign * (pltpu.roll(st, LANES // 2, 1) * ti)
    return jnp.concatenate([sr * rr - si * ri, sr * ri + si * rr, mixed], 1)


def times_conjugate(grad, rel, main, first, sign):
    gr, gi, gt = complex_parts(grad, main)
    rr, ri, rt = complex_parts(rel, main)
    tr, ti = tail_forms(rt, first)
    mixed = gt * tr - sign * (pltpu.roll(gt, LANES // 2, 1) * ti)
    return jnp.concatenate([gr * rr + gi * ri, gi * rr - gr * ri, mixed], 1)


def kernel(
    groups,
    members,
    owners,
    entity,
    state_in,
    relation,
    source_ids,
    relation_ids,
    dest_groups,
    dest_rows,
    negative_ids,
    entity_out,
    state_out,
    place,
    table,
    state,
    rel_table,
    slot_src,
    slot_rel,
    src_rows,
    taken,
    ids_send,
    ids_recv,
    counts,
    rel_slots,
    query,
    neg_exp,
    neg_max,
    neg_sum,
    weights,
    row_send,
    row_recv,
    grad_send,
    grad_recv,
    source_acc,
    grads,
    ar_in,
    ar_half,
    ar_mine,
    ar_parts,
    ar_piece,
    ar_other,
    ar_out,
    ids_ss,
    ids_rs,
    row_ss,
    row_rs,
    grad_ss,
    grad_rs,
    p1_ss,
    p1_rs,
    p2_ss,
    p2_rs,
    p3_ss,
    p3_rs,
    p4_ss,
    p4_rs,
    p5_ss,
    p5_rs,
):
    steps, edges = source_ids.shape
    width, rows = entity.shape
    rel_rows = relation.shape[1]
    half = width // 2
    main = half // LANES * LANES
    wide = table.shape[1]
    slots = groups * CAP
    depth = members // 4
    rings = groups // 2

    g = lax.axis_index("group")
    m = lax.axis_index("member")
    gx, gy = g // rings, g % rings
    core, z, xh = m % 2, (m // 2) % depth, m // (2 * depth)
    twin = m + 1 - 2 * core
    across = (m + 2 * depth) % members

    def peer(k):
        return ((gx + k // rings) % 2) * rings + (gy + k % rings) % rings

    def mirror(k):
        return k // rings * rings + (rings - k % rings) % rings

    def floor(k):
        return (z + k) % depth

    def along(other):
        return (g, xh * (2 * depth) + other * 2 + core)

    def remote(src, dst, send_sem, recv_sem, device):
        return pltpu.make_async_remote_copy(
            src_ref=src,
            dst_ref=dst,
            send_sem=send_sem,
            recv_sem=recv_sem,
            device_id=device,
            device_id_type=MESH,
        )

    barrier = pltpu.get_barrier_semaphore()

    for k in range(1, groups):
        pl.semaphore_signal(barrier, inc=1, device_id=(peer(k), m), device_id_type=MESH)
    for k in range(1, depth):
        pl.semaphore_signal(barrier, inc=1, device_id=along(floor(k)), device_id_type=MESH)
    pl.semaphore_signal(barrier, inc=1, device_id=(g, twin), device_id_type=MESH)
    pl.semaphore_signal(barrier, inc=1, device_id=(g, across), device_id_type=MESH)

    comp = iota((width, 1), 0)
    imag = comp >= half
    local = jnp.where(imag, comp - half, comp)
    spot = jnp.where(
        local < main,
        local + jnp.where(imag, main, 0),
        2 * main + jnp.where(imag, LANES // 2, 0) + local - main,
    )
    place[...] = onehot(iota((width, wide), 1) == spot)
    table[...] = dot_tn(entity[...], place[...]).astype(BF16)
    eye = iota((rows, rows), 0) == iota((rows, rows), 1)
    state[...] = jnp.sum(jnp.where(eye, state_in[...], 0.0), 1, keepdims=True)
    first = iota((1, LANES), 1) < LANES // 2
    sign = jnp.where(first, -1.0, 1.0)

    pl.semaphore_wait(barrier, groups + depth)

    def ids_copy(k):
        return remote(
            ids_send.at[k], ids_recv.at[mirror(k)], ids_ss.at[k], ids_rs.at[mirror(k)], (peer(k), m)
        )

    def ids_arrival(k):
        return remote(ids_send.at[k], ids_recv.at[k], ids_ss.at[k], ids_rs.at[k], (peer(k), m))

    def edge_facts(s):
        rel_row = relation_ids[s : s + 1, :]
        high = rel_row // 32
        which = iota((16, edges), 0)
        facts = jnp.where(which == 0, source_ids[s : s + 1, :], 0)
        facts = jnp.where(which == 1, high, facts)
        facts = jnp.where(which == 2, rel_row - 32 * high, facts)
        facts = jnp.where(which == 3, dest_rows[s : s + 1, :], facts)
        facts = jnp.where(which == 4, 1, facts)
        return facts.astype(F32).astype(BF16)

    def assign_slots():
        ids_send[...] = jnp.zeros_like(ids_send)
        before = onehot(iota((edges, edges), 0) < iota((edges, edges), 1))
        for s in range(steps):
            group_row = dest_groups[s]
            hop_x = (group_row // rings + 2 - gx) % 2
            hop_y = (group_row % rings + rings - gy) % rings
            hop = hop_x * rings + hop_y
            named = iota((16, edges), 0) == hop
            rank = dot_nn(onehot(named), before)
            rank = jnp.sum(jnp.where(named, rank, 0.0), 0, keepdims=True)
            slot_row = hop * CAP + rank.astype(jnp.int32)
            taken[s] = onehot(iota((slots, edges), 0) == slot_row)
            flat = dot_nt(edge_facts(s), taken[s]).astype(jnp.int32)
            empty = flat[4:5, :] - 1
            src_rows[s] = flat[0:1, :] + 4 * rows * empty
            wanted = flat[3:4, :] + 4 * rows * empty
            for k in range(groups):
                ids_send[k, s : s + 1, :] = wanted[:, k * CAP : (k + 1) * CAP]
        for k in range(1, groups):
            ids_copy(k).start()
        ids_recv[0] = ids_send[0]

    def slot_columns():
        for s in range(steps):
            tall = dot_nt(taken[s], edge_facts(s)).astype(jnp.int32)
            empty = tall[:, 4:5] - 1
            slot_src[s] = tall[:, 0:1] + 4 * rows * empty
            slot_rel[s] = 32 * tall[:, 1:2] + tall[:, 2:3] + 4 * rel_rows * empty

    def ids_wait():
        for k in range(1, groups):
            ids_copy(k).wait_send()
            ids_arrival(k).wait_recv()

    def ar_first(i):
        return remote(
            ar_in.at[i, 1 - core], ar_half.at[i], p1_ss.at[i], p1_rs.at[i], (g, twin)
        )

    def ar_scatter_copy(i, other):
        return remote(
            ar_mine.at[i, other],
            ar_parts.at[i, z],
            p2_ss.at[i, other],
            p2_rs.at[i, z],
            along(other),
        )

    def ar_scatter_arrival(i, other):
        return remote(
            ar_mine.at[i, other],
            ar_parts.at[i, other],
            p2_ss.at[i, other],
            p2_rs.at[i, other],
            along(other),
        )

    def ar_cross_copy(i):
        return remote(ar_piece.at[i], ar_other.at[i], p3_ss.at[i], p3_rs.at[i], (g, across))

    def ar_gather_copy(i, other):
        return remote(
            ar_out.at[i, core, z],
            ar_out.at[i, core, z],
            p4_ss.at[i, other],
            p4_rs.at[i, z],
            along(other),
        )

    def ar_gather_arrival(i, other):
        return remote(
            ar_out.at[i, core, other],
            ar_out.at[i, core, other],
            p4_ss.at[i, other],
            p4_rs.at[i, other],
            along(other),
        )

    def ar_last(i, which):
        return remote(
            ar_out.at[i, which], ar_out.at[i, which], p5_ss.at[i], p5_rs.at[i], (g, twin)
        )

    def ar_scatter(i):
        ar_first(i).wait()
        mine = ar_in[i, core].astype(F32) + ar_half[i].astype(F32)
        ar_mine[i] = mine.astype(BF16).reshape(depth, rows // 2 // depth, wide)

        @pl.loop(1, depth)
        def _(k):
            ar_scatter_copy(i, floor(k)).start()

    def ar_cross(i):
        @pl.loop(1, depth)
        def _(k):
            other = floor(k)
            ar_scatter_copy(i, other).wait_send()
            ar_scatter_arrival(i, other).wait_recv()

        ar_parts[i, z] = ar_mine[i, z]
        piece = jnp.sum(ar_parts[i].astype(F32), 0)
        ar_piece[i] = piece.astype(BF16)
        ar_cross_copy(i).start()

    def ar_gather(i):
        ar_cross_copy(i).wait()
        whole = ar_piece[i].astype(F32) + ar_other[i].astype(F32)
        ar_out[i, core, z] = whole.astype(BF16)

        @pl.loop(1, depth)
        def _(k):
            ar_gather_copy(i, floor(k)).start()

    def ar_share(i):
        @pl.loop(1, depth)
        def _(k):
            other = floor(k)
            ar_gather_copy(i, other).wait_send()
            ar_gather_arrival(i, other).wait_recv()

        ar_last(i, core).start()

    def ar_done(i):
        ar_last(i, core).wait_send()
        ar_last(i, 1 - core).wait_recv()

    @pl.loop(0, steps)
    def _(s):
        root = owners[s, g]
        fetch, reduce = 2 * s, 2 * s + 1

        def row_copy(k):
            return remote(
                row_send.at[s, k],
                row_recv.at[s, mirror(k)],
                row_ss.at[s, k],
                row_rs.at[s, mirror(k)],
                (peer(k), m),
            )

        def row_arrival(k):
            return remote(
                row_send.at[s, k], row_recv.at[s, k], row_ss.at[s, k], row_rs.at[s, k], (peer(k), m)
            )

        def grad_copy(k):
            return remote(
                grad_send.at[s, k],
                grad_recv.at[s, mirror(k)],
                grad_ss.at[s, k],
                grad_rs.at[s, mirror(k)],
                (peer(k), m),
            )

        def grad_arrival(k):
            return remote(
                grad_send.at[s, k],
                grad_recv.at[s, k],
                grad_ss.at[s, k],
                grad_rs.at[s, k],
                (peer(k), m),
            )

        def asked(p):
            ids = [ids_recv[2 * p + j, pl.ds(s, 1), :] for j in range(2)]
            return onehot(iota((rows, 2 * CAP), 0) == jnp.concatenate(ids, 1))

        def pick_rows(p):
            picked = dot_tn(asked(p), table[...]).astype(BF16)
            row_send[s, 2 * p : 2 * p + 2] = picked.reshape(2, CAP, wide)

        def send_rows(p):
            for k in (2 * p, 2 * p + 1):
                if k:
                    row_copy(k).start()

        def relations(k):
            base = pl.multiple_of(k * 2 * CAP, 2 * CAP)
            chosen = onehot(iota((2 * CAP, rel_rows), 1) == slot_rel[s, pl.ds(base, 2 * CAP), :])
            rel_slots[pl.ds(base, 2 * CAP), :] = dot_nn(chosen, rel_table[...]).astype(BF16)

        ar_in[fetch] = (
            jnp.where(m == root, table[...].astype(F32), 0.0).astype(BF16)
        ).reshape(2, rows // 2, wide)
        ar_first(fetch).start()

        @pl.when(s == 0)
        def _():
            assign_slots()

        @pl.when(s > 0)
        def _():
            pick_rows(2)
            send_rows(2)

        ar_scatter(fetch)

        @pl.when(s == 0)
        def _():
            slot_columns()
            ids_wait()
            pick_rows(2)
            send_rows(2)

        pick_rows(0)
        send_rows(0)
        row_recv[s, 0] = row_send[s, 0]
        pick_rows(1)
        send_rows(1)
        pick_rows(3)

        @pl.when(s == 0)
        def _():
            rel_table[...] = dot_tn(relation[...], place[...]).astype(BF16)

        slot_count = negative_ids.shape[1]
        hits = onehot(iota((rows, slot_count), 0) == negative_ids[pl.ds(s, 1), :])
        counts[...] = dot_nt(jnp.ones((8, slot_count), BF16), hits)
        ar_cross(fetch)
        send_rows(3)

        @pl.loop(0, groups // 4)
        def _(k):
            relations(k)

        ar_gather(fetch)

        @pl.loop(groups // 4, groups // 2)
        def _(k):
            relations(k)

        ar_share(fetch)
        source_acc[...] = jnp.zeros_like(source_acc)
        count_row = counts[0:1, :]
        present = count_row > 0.5
        ar_done(fetch)

        @pl.loop(0, groups // 2)
        def _(p):
            base = pl.multiple_of(p * 2 * CAP, 2 * CAP)
            here = pl.ds(base, 2 * CAP)
            chosen = onehot(iota((2 * CAP, rows), 1) == slot_src[s, here, :])
            source = dot_nn(chosen, ar_out[fetch].reshape(rows, wide))
            q = times(source, rel_slots[here, :].astype(F32), main, first, sign).astype(BF16)
            query[here, :] = q
            scores = jnp.where(present, dot_nt(q, table[...]), LOW)
            top = jnp.max(scores, 1, keepdims=True)
            e = jnp.exp(scores - top) * count_row
            neg_exp[here, :] = e
            neg_max[here, :] = top
            neg_sum[here, :] = jnp.sum(e, 1, keepdims=True)

        @pl.loop(0, groups // 2)
        def _(turn):
            p = (turn + 2) % 3 * (1 - turn // 3) + turn // 3 * 3

            for j in range(2):

                @pl.when(2 * p + j > 0)
                def _():
                    row_copy(2 * p + j).wait_send()
                    row_arrival(2 * p + j).wait_recv()

            base = pl.multiple_of(p * 2 * CAP, 2 * CAP)
            here = pl.ds(base, 2 * CAP)
            pair = pl.ds(2 * p, 2)
            q = query[here, :].astype(F32)
            dest = row_recv[s, pair].reshape(2 * CAP, wide).astype(F32)
            positive = jnp.sum(q * dest, 1, keepdims=True)
            low = neg_max[here, :]
            top = jnp.maximum(low, positive)
            pos_exp = jnp.exp(positive - top)
            shrink = jnp.exp(low - top)
            total = pos_exp + neg_sum[here, :] * shrink
            coef_pos = pos_exp / total - 1.0
            grad_send[s, pair] = (coef_pos * q).astype(BF16).reshape(2, CAP, wide)

            for j in range(2):

                @pl.when((2 * p + j > 0) & (p < 3))
                def _():
                    grad_copy(2 * p + j).start()

            coef_neg = (neg_exp[here, :] * (shrink / total)).astype(BF16)
            weights[here, :] = coef_neg
            grad_query = coef_pos * dest + dot_nn(coef_neg, table[...])
            grad_source = times_conjugate(
                grad_query, rel_slots[here, :].astype(F32), main, first, sign
            ).astype(BF16)
            spread = onehot(iota((rows, 2 * CAP), 0) == src_rows[s, :, here])
            source_acc[...] += dot_nn(spread, grad_source)

        ar_in[reduce] = source_acc[...].astype(BF16).reshape(2, rows // 2, wide)
        ar_first(reduce).start()
        grad_recv[s, 0] = grad_send[s, 0]
        ar_scatter(reduce)
        grads[...] = dot_tn(weights[...], query[...])
        ar_cross(reduce)
        grad_copy(6).start()
        grad_copy(7).start()
        ar_gather(reduce)

        def scatter_grads(p):
            for k in (2 * p, 2 * p + 1):
                if k:
                    grad_copy(k).wait_send()
                    grad_arrival(k).wait_recv()
            arrived = grad_recv[s, 2 * p : 2 * p + 2].reshape(2 * CAP, wide)
            grads[...] += dot_nn(asked(p), arrived)

        scatter_grads(2)
        scatter_grads(0)
        scatter_grads(1)
        ar_share(reduce)
        scatter_grads(3)
        ar_done(reduce)
        total = grads[...] + jnp.where(
            m == root, ar_out[reduce].reshape(rows, wide).astype(F32), 0.0
        )
        fresh = state[...] + jnp.sum(total * total, 1, keepdims=True) * (1.0 / width)
        state[...] = fresh
        table[...] = (table[...].astype(F32) - total / jnp.sqrt(fresh)).astype(BF16)

    entity_out[...] = dot_nt(place[...], table[...]).astype(BF16)
    state_out[...] = jnp.sum(jnp.where(eye, state[...], 0.0), 0, keepdims=True)


def per_device(
    groups,
    members,
    entity,
    adagrad_state,
    relation,
    source_ids,
    relation_ids,
    dest_groups,
    dest_rows,
    negative_ids,
    owners,
):
    rows, width = entity.shape
    steps, edges = source_ids.shape
    half = width // 2
    wide = 2 * (half // LANES * LANES) + LANES
    slots = groups * CAP
    depth = members // 4
    piece = rows // 2 // depth
    uses = 2 * steps
    dma = pltpu.SemaphoreType.DMA
    vmem = pltpu.VMEM
    whole = pl.BlockSpec(memory_space=pltpu.VMEM)
    table, state = pl.pallas_call(
        functools.partial(kernel, groups, members),
        out_shape=(
            jax.ShapeDtypeStruct((width, rows), BF16),
            jax.ShapeDtypeStruct((1, rows), F32),
        ),
        in_specs=[pl.BlockSpec(memory_space=pltpu.SMEM)] + [whole] * 8,
        out_specs=(whole, whole),
        scratch_shapes=[
            vmem((width, wide), BF16),
            vmem((rows, wide), BF16),
            vmem((rows, 1), F32),
            vmem((relation.shape[0], wide), BF16),
            vmem((steps, slots, 1), jnp.int32),
            vmem((steps, slots, 1), jnp.int32),
            vmem((steps, 1, slots), jnp.int32),
            vmem((steps, slots, edges), BF16),
            vmem((groups, 8, CAP), jnp.int32),
            vmem((groups, 8, CAP), jnp.int32),
            vmem((8, rows), F32),
            vmem((slots, wide), BF16),
            vmem((slots, wide), BF16),
            vmem((slots, rows), F32),
            vmem((slots, 1), F32),
            vmem((slots, 1), F32),
            vmem((slots, rows), BF16),
            vmem((steps, groups, CAP, wide), BF16),
            vmem((steps, groups, CAP, wide), BF16),
            vmem((steps, groups, CAP, wide), BF16),
            vmem((steps, groups, CAP, wide), BF16),
            vmem((rows, wide), F32),
            vmem((rows, wide), F32),
            vmem((uses, 2, rows // 2, wide), BF16),
            vmem((uses, rows // 2, wide), BF16),
            vmem((uses, depth, piece, wide), BF16),
            vmem((uses, depth, piece, wide), BF16),
            vmem((uses, piece, wide), BF16),
            vmem((uses, piece, wide), BF16),
            vmem((uses, 2, depth, piece, wide), BF16),
            dma((groups,)),
            dma((groups,)),
            dma((steps, groups)),
            dma((steps, groups)),
            dma((steps, groups)),
            dma((steps, groups)),
            dma((uses,)),
            dma((uses,)),
            dma((uses, depth)),
            dma((uses, depth)),
            dma((uses,)),
            dma((uses,)),
            dma((uses, depth)),
            dma((uses, depth)),
            dma((uses,)),
            dma((uses,)),
        ],
        compiler_params=pltpu.CompilerParams(
            collective_id=0, has_side_effects=True, vmem_limit_bytes=60 << 20
        ),
    )(
        owners,
        entity.T,
        adagrad_state.reshape(1, rows),
        relation.T,
        source_ids,
        relation_ids,
        jnp.transpose(dest_groups, (0, 2, 1)),
        dest_rows,
        negative_ids,
    )
    return (table.T, state.reshape(rows))


def solution(mesh):
    placed = (
        P(("group", "member"), None),
        P(("group", "member")),
        P(),
        P(None, ("group", "member")),
        P(None, ("group", "member")),
        P(None, ("group", "member"), None),
        P(None, ("group", "member")),
        P(None, ("group", "member")),
        P(),
    )
    return jax.shard_map(
        functools.partial(per_device, mesh.shape["group"], mesh.shape["member"]),
        mesh=mesh,
        in_specs=placed,
        out_specs=(P(("group", "member"), None), P(("group", "member"))),
        check_vma=False,
    )
```

```python
import functools

import jax
import jax.numpy as jnp
from jax import lax
from jax.experimental import pallas as pl
from jax.experimental.pallas import tpu as pltpu
from jax.sharding import PartitionSpec as P

MESH = pl.DeviceIdType.MESH
F32 = jnp.float32
BF16 = jnp.bfloat16
LANES = 128
CAP = 128
LOW = -1e30


def dot_nn(a, b):
    return lax.dot_general(a, b, (((1,), (0,)), ((), ())), preferred_element_type=F32)


def dot_nt(a, b):
    return lax.dot_general(a, b, (((1,), (1,)), ((), ())), preferred_element_type=F32)


def dot_tn(a, b):
    return lax.dot_general(a, b, (((0,), (0,)), ((), ())), preferred_element_type=F32)


def iota(shape, dim):
    return lax.broadcasted_iota(jnp.int32, shape, dim)


def onehot(mask):
    return jnp.where(mask, 1.0, 0.0).astype(BF16)


def complex_parts(value, main):
    return value[:, :main], value[:, main : 2 * main], value[:, 2 * main :]


def tail_forms(tail, first):
    swapped = pltpu.roll(tail, LANES // 2, 1)
    return jnp.where(first, tail, swapped), jnp.where(first, swapped, tail)


def times(source, rel, main, first, sign):
    sr, si, st = complex_parts(source, main)
    rr, ri, rt = complex_parts(rel, main)
    tr, ti = tail_forms(rt, first)
    mixed = st * tr + sign * (pltpu.roll(st, LANES // 2, 1) * ti)
    return jnp.concatenate([sr * rr - si * ri, sr * ri + si * rr, mixed], 1)


def times_conjugate(grad, rel, main, first, sign):
    gr, gi, gt = complex_parts(grad, main)
    rr, ri, rt = complex_parts(rel, main)
    tr, ti = tail_forms(rt, first)
    mixed = gt * tr - sign * (pltpu.roll(gt, LANES // 2, 1) * ti)
    return jnp.concatenate([gr * rr + gi * ri, gi * rr - gr * ri, mixed], 1)


def pack(value, main, tail):
    count = value.shape[0]
    part = count // (LANES // 2 // tail)
    tiles = [value[:, c : c + LANES] for c in range(0, 2 * main, LANES)]
    last = value[:, 2 * main :]
    mixed = last[:part]
    for j in range(1, count // part):
        mixed = mixed + pltpu.roll(last[j * part : (j + 1) * part], tail * j, 1)
    return jnp.concatenate(tiles + [mixed], 0)


def unpack(stack, count, main, tail):
    part = count // (LANES // 2 // tail)
    tiles = 2 * main // LANES
    mixed = stack[tiles * count : tiles * count + part]
    used = iota((1, LANES), 1) % (LANES // 2) < tail
    last = [jnp.where(used, mixed, 0.0)]
    for j in range(1, count // part):
        last.append(jnp.where(used, pltpu.roll(mixed, LANES - tail * j, 1), 0.0))
    columns = [stack[c * count : (c + 1) * count] for c in range(tiles)]
    return jnp.concatenate(columns + [jnp.concatenate(last, 0)], 1)


def kernel(
    groups,
    members,
    owners,
    entity,
    state_in,
    relation,
    source_ids,
    relation_ids,
    dest_groups,
    dest_rows,
    negative_ids,
    entity_out,
    state_out,
    place,
    table,
    state,
    rel_table,
    slot_src,
    slot_rel,
    src_rows,
    taken,
    ids_send,
    ids_recv,
    counts,
    rel_slots,
    query,
    neg_exp,
    neg_max,
    neg_sum,
    weights,
    row_send,
    row_recv,
    grad_send,
    grad_recv,
    block,
    source_acc,
    grads,
    ar_in,
    ar_half,
    ar_mine,
    ar_parts,
    ar_piece,
    ar_other,
    ar_out,
    ids_ss,
    ids_rs,
    row_ss,
    row_rs,
    grad_ss,
    grad_rs,
    p1_ss,
    p1_rs,
    p2_ss,
    p2_rs,
    p3_ss,
    p3_rs,
    p4_ss,
    p4_rs,
    p5_ss,
    p5_rs,
):
    steps, edges = source_ids.shape
    width, rows = entity.shape
    rel_rows = relation.shape[1]
    half = width // 2
    main = half // LANES * LANES
    wide = table.shape[1]
    tail = half - main
    share = rows // 2
    piece = ar_half.shape[2]
    slots = groups * CAP
    depth = members // 4
    rings = groups // 2

    g = lax.axis_index("group")
    m = lax.axis_index("member")
    gx, gy = g // rings, g % rings
    core, z, xh = m % 2, (m // 2) % depth, m // (2 * depth)
    twin = m + 1 - 2 * core
    across = (m + 2 * depth) % members

    def peer(k):
        return ((gx + k // rings) % 2) * rings + (gy + k % rings) % rings

    def mirror(k):
        return k // rings * rings + (rings - k % rings) % rings

    def floor(k):
        return (z + k) % depth

    def along(other):
        return (g, xh * (2 * depth) + other * 2 + core)

    def remote(src, dst, send_sem, recv_sem, device):
        return pltpu.make_async_remote_copy(
            src_ref=src,
            dst_ref=dst,
            send_sem=send_sem,
            recv_sem=recv_sem,
            device_id=device,
            device_id_type=MESH,
        )

    barrier = pltpu.get_barrier_semaphore()

    for k in range(1, groups):
        pl.semaphore_signal(barrier, inc=1, device_id=(peer(k), m), device_id_type=MESH)
    for k in range(1, depth):
        pl.semaphore_signal(barrier, inc=1, device_id=along(floor(k)), device_id_type=MESH)
    pl.semaphore_signal(barrier, inc=1, device_id=(g, twin), device_id_type=MESH)
    pl.semaphore_signal(barrier, inc=1, device_id=(g, across), device_id_type=MESH)

    comp = iota((width, 1), 0)
    imag = comp >= half
    local = jnp.where(imag, comp - half, comp)
    spot = jnp.where(
        local < main,
        local + jnp.where(imag, main, 0),
        2 * main + jnp.where(imag, LANES // 2, 0) + local - main,
    )
    place[...] = onehot(iota((width, wide), 1) == spot)
    table[...] = dot_tn(entity[...], place[...]).astype(BF16)
    eye = iota((rows, rows), 0) == iota((rows, rows), 1)
    state[...] = jnp.sum(jnp.where(eye, state_in[...], 0.0), 1, keepdims=True)
    first = iota((1, LANES), 1) < LANES // 2
    sign = jnp.where(first, -1.0, 1.0)

    def ids_copy(k):
        return remote(
            ids_send.at[k], ids_recv.at[mirror(k)], ids_ss.at[k], ids_rs.at[mirror(k)], (peer(k), m)
        )

    def ids_arrival(k):
        return remote(ids_send.at[k], ids_recv.at[k], ids_ss.at[k], ids_rs.at[k], (peer(k), m))

    def edge_facts(s):
        rel_row = relation_ids[s : s + 1, :]
        high = rel_row // 32
        which = iota((16, edges), 0)
        facts = jnp.where(which == 0, source_ids[s : s + 1, :], 0)
        facts = jnp.where(which == 1, high, facts)
        facts = jnp.where(which == 2, rel_row - 32 * high, facts)
        facts = jnp.where(which == 3, dest_rows[s : s + 1, :], facts)
        facts = jnp.where(which == 4, 1, facts)
        return facts.astype(F32).astype(BF16)

    def assign_slots():
        ids_send[...] = jnp.zeros_like(ids_send)
        before = onehot(iota((edges, edges), 0) < iota((edges, edges), 1))
        for s in range(steps):
            group_row = dest_groups[s]
            hop_x = (group_row // rings + 2 - gx) % 2
            hop_y = (group_row % rings + rings - gy) % rings
            hop = hop_x * rings + hop_y
            named = iota((16, edges), 0) == hop
            rank = dot_nn(onehot(named), before)
            rank = jnp.sum(jnp.where(named, rank, 0.0), 0, keepdims=True)
            slot_row = hop * CAP + rank.astype(jnp.int32)
            taken[s] = onehot(iota((slots, edges), 0) == slot_row)
            flat = dot_nt(edge_facts(s), taken[s]).astype(jnp.int32)
            empty = flat[4:5, :] - 1
            src_rows[s] = flat[0:1, :] + 4 * rows * empty
            wanted = flat[3:4, :] + 4 * rows * empty
            for k in range(groups):
                ids_send[k, s : s + 1, :] = wanted[:, k * CAP : (k + 1) * CAP]

    assign_slots()
    pl.semaphore_wait(barrier, groups + depth)
    for k in range(1, groups):
        ids_copy(k).start()
    ids_recv[0] = ids_send[0]

    def slot_columns():
        for s in range(steps):
            tall = dot_nt(taken[s], edge_facts(s)).astype(jnp.int32)
            empty = tall[:, 4:5] - 1
            slot_src[s] = tall[:, 0:1] + 4 * rows * empty
            slot_rel[s] = 32 * tall[:, 1:2] + tall[:, 2:3] + 4 * rel_rows * empty

    def ids_wait():
        for k in range(1, groups):
            ids_copy(k).wait_send()
            ids_arrival(k).wait_recv()

    near = sorted(range(1, depth), key=lambda k: min(k, depth - k))
    far = near[::-1]

    def ar_fill(i, value):
        for h in range(2):
            stack = pack(value[h * share : (h + 1) * share], main, tail)
            spare = jnp.zeros((depth * piece - stack.shape[0], LANES), F32)
            stack = jnp.concatenate([stack, spare], 0)
            ar_in[i, h] = stack.reshape(depth, piece, LANES).astype(BF16)

    def ar_read(i):
        halves = []
        for h in range(2):
            stack = ar_out[i, h].astype(F32).reshape(depth * piece, LANES)
            halves.append(unpack(stack, share, main, tail))
        return jnp.concatenate(halves, 0)

    def ar_first_copy(i, other):
        return remote(
            ar_in.at[i, 1 - core, other],
            ar_half.at[i, other],
            p1_ss.at[i, other],
            p1_rs.at[i, other],
            (g, twin),
        )

    def ar_first(i):
        for k in far + [0]:
            ar_first_copy(i, floor(k)).start()

    def ar_scatter_copy(i, other):
        return remote(
            ar_mine.at[i, other],
            ar_parts.at[i, z],
            p2_ss.at[i, other],
            p2_rs.at[i, z],
            along(other),
        )

    def ar_scatter_arrival(i, other):
        return remote(
            ar_mine.at[i, other],
            ar_parts.at[i, other],
            p2_ss.at[i, other],
            p2_rs.at[i, other],
            along(other),
        )

    def ar_cross_copy(i):
        return remote(ar_piece.at[i], ar_other.at[i], p3_ss.at[i], p3_rs.at[i], (g, across))

    def ar_gather_copy(i, other):
        return remote(
            ar_out.at[i, core, z],
            ar_out.at[i, core, z],
            p4_ss.at[i, other],
            p4_rs.at[i, z],
            along(other),
        )

    def ar_gather_arrival(i, other):
        return remote(
            ar_out.at[i, core, other],
            ar_out.at[i, core, other],
            p4_ss.at[i, other],
            p4_rs.at[i, other],
            along(other),
        )

    def ar_last(i, which, other):
        return remote(
            ar_out.at[i, which, other],
            ar_out.at[i, which, other],
            p5_ss.at[i, other],
            p5_rs.at[i, other],
            (g, twin),
        )

    def ar_scatter(i):
        for k in far + [0]:
            other = floor(k)
            ar_first_copy(i, other).wait()
            mine = ar_in[i, core, other].astype(F32) + ar_half[i, other].astype(F32)
            ar_mine[i, other] = mine.astype(BF16)
            if k:
                ar_scatter_copy(i, other).start()

    def ar_cross(i):
        @pl.loop(1, depth)
        def _(k):
            other = floor(k)
            ar_scatter_copy(i, other).wait_send()
            ar_scatter_arrival(i, other).wait_recv()

        ar_parts[i, z] = ar_mine[i, z]
        piece = jnp.sum(ar_parts[i].astype(F32), 0)
        ar_piece[i] = piece.astype(BF16)
        ar_cross_copy(i).start()

    def ar_gather(i):
        ar_cross_copy(i).wait()
        whole = ar_piece[i].astype(F32) + ar_other[i].astype(F32)
        ar_out[i, core, z] = whole.astype(BF16)
        for k in far:
            ar_gather_copy(i, floor(k)).start()
        ar_last(i, core, z).start()

    def ar_share(i):
        for k in near:
            other = floor(k)
            ar_gather_arrival(i, other).wait_recv()
            ar_last(i, core, other).start()

    def ar_done(i):
        for k in [0] + near:
            other = floor(k)
            if k:
                ar_gather_copy(i, other).wait_send()
            ar_last(i, core, other).wait_send()
            ar_last(i, 1 - core, other).wait_recv()

    @pl.loop(0, steps)
    def _(s):
        root = owners[s, g]
        fetch, reduce = 2 * s, 2 * s + 1

        def row_copy(k):
            return remote(
                row_send.at[s, k],
                row_recv.at[s, mirror(k)],
                row_ss.at[s, k],
                row_rs.at[s, mirror(k)],
                (peer(k), m),
            )

        def row_arrival(k):
            return remote(
                row_send.at[s, k], row_recv.at[s, k], row_ss.at[s, k], row_rs.at[s, k], (peer(k), m)
            )

        def grad_copy(k):
            return remote(
                grad_send.at[s, k],
                grad_recv.at[s, mirror(k)],
                grad_ss.at[s, k],
                grad_rs.at[s, mirror(k)],
                (peer(k), m),
            )

        def grad_arrival(k):
            return remote(
                grad_send.at[s, k],
                grad_recv.at[s, k],
                grad_ss.at[s, k],
                grad_rs.at[s, k],
                (peer(k), m),
            )

        def asked(p):
            ids = [ids_recv[2 * p + j, pl.ds(s, 1), :] for j in range(2)]
            return onehot(iota((rows, 2 * CAP), 0) == jnp.concatenate(ids, 1))

        def pick_rows(p):
            picked = dot_tn(asked(p), table[...])
            for j in range(2):
                row_send[s, 2 * p + j] = pack(picked[j * CAP : (j + 1) * CAP], main, tail).astype(BF16)

        def send_rows(p):
            for k in (2 * p, 2 * p + 1):
                if k:
                    row_copy(k).start()

        def relations(k):
            base = pl.multiple_of(k * 2 * CAP, 2 * CAP)
            chosen = onehot(iota((2 * CAP, rel_rows), 1) == slot_rel[s, pl.ds(base, 2 * CAP), :])
            rel_slots[pl.ds(base, 2 * CAP), :] = dot_nn(chosen, rel_table[...]).astype(BF16)

        ar_fill(fetch, jnp.where(m == root, table[...].astype(F32), 0.0))
        ar_first(fetch)

        @pl.when(s > 0)
        def _():
            pick_rows(2)
            send_rows(2)

        ar_scatter(fetch)

        @pl.when(s == 0)
        def _():
            slot_columns()
            ids_wait()
            pick_rows(2)
            send_rows(2)

        pick_rows(0)
        send_rows(0)
        row_recv[s, 0] = row_send[s, 0]
        pick_rows(1)
        send_rows(1)
        pick_rows(3)

        @pl.when(s == 0)
        def _():
            rel_table[...] = dot_tn(relation[...], place[...]).astype(BF16)

        slot_count = negative_ids.shape[1]
        hits = onehot(iota((rows, slot_count), 0) == negative_ids[pl.ds(s, 1), :])
        counts[...] = dot_nt(jnp.ones((8, slot_count), BF16), hits)
        ar_cross(fetch)
        send_rows(3)

        @pl.loop(0, groups // 4)
        def _(k):
            relations(k)

        ar_gather(fetch)

        @pl.loop(groups // 4, groups // 2)
        def _(k):
            relations(k)

        ar_share(fetch)
        source_acc[...] = jnp.zeros_like(source_acc)
        count_row = counts[0:1, :]
        present = count_row > 0.5
        ar_done(fetch)
        block[...] = ar_read(fetch).astype(BF16)

        @pl.loop(0, groups // 2)
        def _(p):
            base = pl.multiple_of(p * 2 * CAP, 2 * CAP)
            here = pl.ds(base, 2 * CAP)
            chosen = onehot(iota((2 * CAP, rows), 1) == slot_src[s, here, :])
            source = dot_nn(chosen, block[...])
            q = times(source, rel_slots[here, :].astype(F32), main, first, sign).astype(BF16)
            query[here, :] = q
            scores = jnp.where(present, dot_nt(q, table[...]), LOW)
            top = jnp.max(scores, 1, keepdims=True)
            e = jnp.exp(scores - top) * count_row
            neg_exp[here, :] = e
            neg_max[here, :] = top
            neg_sum[here, :] = jnp.sum(e, 1, keepdims=True)

        @pl.loop(0, groups // 2)
        def _(turn):
            p = (turn + 2) % 3 * (1 - turn // 3) + turn // 3 * 3

            for j in range(2):

                @pl.when(2 * p + j > 0)
                def _():
                    row_copy(2 * p + j).wait_send()
                    row_arrival(2 * p + j).wait_recv()

            base = pl.multiple_of(p * 2 * CAP, 2 * CAP)
            here = pl.ds(base, 2 * CAP)
            q = query[here, :].astype(F32)
            dest = jnp.concatenate(
                [unpack(row_recv[s, 2 * p + j].astype(F32), CAP, main, tail) for j in range(2)], 0
            )
            positive = jnp.sum(q * dest, 1, keepdims=True)
            low = neg_max[here, :]
            top = jnp.maximum(low, positive)
            pos_exp = jnp.exp(positive - top)
            shrink = jnp.exp(low - top)
            total = pos_exp + neg_sum[here, :] * shrink
            coef_pos = pos_exp / total - 1.0
            grad_dest = coef_pos * q
            for j in range(2):
                stack = pack(grad_dest[j * CAP : (j + 1) * CAP], main, tail)
                grad_send[s, 2 * p + j] = stack.astype(BF16)

            for j in range(2):

                @pl.when((2 * p + j > 0) & (p < 3))
                def _():
                    grad_copy(2 * p + j).start()

            coef_neg = (neg_exp[here, :] * (shrink / total)).astype(BF16)
            weights[here, :] = coef_neg
            grad_query = coef_pos * dest + dot_nn(coef_neg, table[...])
            grad_source = times_conjugate(
                grad_query, rel_slots[here, :].astype(F32), main, first, sign
            ).astype(BF16)
            spread = onehot(iota((rows, 2 * CAP), 0) == src_rows[s, :, here])
            source_acc[...] += dot_nn(spread, grad_source)

        ar_fill(reduce, source_acc[...])
        ar_first(reduce)
        grad_recv[s, 0] = grad_send[s, 0]
        ar_scatter(reduce)
        grads[...] = dot_tn(weights[...], query[...])
        ar_cross(reduce)
        grad_copy(6).start()
        grad_copy(7).start()
        ar_gather(reduce)

        def scatter_grads(p):
            for k in (2 * p, 2 * p + 1):
                if k:
                    grad_copy(k).wait_send()
                    grad_arrival(k).wait_recv()
            arrived = [unpack(grad_recv[s, k].astype(F32), CAP, main, tail) for k in (2 * p, 2 * p + 1)]
            grads[...] += dot_nn(asked(p), jnp.concatenate(arrived, 0).astype(BF16))

        scatter_grads(2)
        scatter_grads(0)
        scatter_grads(1)
        ar_share(reduce)
        scatter_grads(3)
        ar_done(reduce)
        total = grads[...] + jnp.where(m == root, ar_read(reduce), 0.0)
        fresh = state[...] + jnp.sum(total * total, 1, keepdims=True) * (1.0 / width)
        state[...] = fresh
        table[...] = (table[...].astype(F32) - total / jnp.sqrt(fresh)).astype(BF16)

    entity_out[...] = dot_nt(place[...], table[...]).astype(BF16)
    state_out[...] = jnp.sum(jnp.where(eye, state[...], 0.0), 0, keepdims=True)


def per_device(
    groups,
    members,
    entity,
    adagrad_state,
    relation,
    source_ids,
    relation_ids,
    dest_groups,
    dest_rows,
    negative_ids,
    owners,
):
    rows, width = entity.shape
    steps, edges = source_ids.shape
    half = width // 2
    wide = 2 * (half // LANES * LANES) + LANES
    slots = groups * CAP
    depth = members // 4
    stack = CAP * width // LANES
    piece = -(-rows // 2 * width // LANES // depth // 8) * 8
    uses = 2 * steps
    dma = pltpu.SemaphoreType.DMA
    vmem = pltpu.VMEM
    whole = pl.BlockSpec(memory_space=pltpu.VMEM)
    table, state = pl.pallas_call(
        functools.partial(kernel, groups, members),
        out_shape=(
            jax.ShapeDtypeStruct((width, rows), BF16),
            jax.ShapeDtypeStruct((1, rows), F32),
        ),
        in_specs=[pl.BlockSpec(memory_space=pltpu.SMEM)] + [whole] * 8,
        out_specs=(whole, whole),
        scratch_shapes=[
            vmem((width, wide), BF16),
            vmem((rows, wide), BF16),
            vmem((rows, 1), F32),
            vmem((relation.shape[0], wide), BF16),
            vmem((steps, slots, 1), jnp.int32),
            vmem((steps, slots, 1), jnp.int32),
            vmem((steps, 1, slots), jnp.int32),
            vmem((steps, slots, edges), BF16),
            vmem((groups, 8, CAP), jnp.int32),
            vmem((groups, 8, CAP), jnp.int32),
            vmem((8, rows), F32),
            vmem((slots, wide), BF16),
            vmem((slots, wide), BF16),
            vmem((slots, rows), F32),
            vmem((slots, 1), F32),
            vmem((slots, 1), F32),
            vmem((slots, rows), BF16),
            vmem((steps, groups, stack, LANES), BF16),
            vmem((steps, groups, stack, LANES), BF16),
            vmem((steps, groups, stack, LANES), BF16),
            vmem((steps, groups, stack, LANES), BF16),
            vmem((rows, wide), BF16),
            vmem((rows, wide), F32),
            vmem((rows, wide), F32),
            vmem((uses, 2, depth, piece, LANES), BF16),
            vmem((uses, depth, piece, LANES), BF16),
            vmem((uses, depth, piece, LANES), BF16),
            vmem((uses, depth, piece, LANES), BF16),
            vmem((uses, piece, LANES), BF16),
            vmem((uses, piece, LANES), BF16),
            vmem((uses, 2, depth, piece, LANES), BF16),
            dma((groups,)),
            dma((groups,)),
            dma((steps, groups)),
            dma((steps, groups)),
            dma((steps, groups)),
            dma((steps, groups)),
            dma((uses, depth)),
            dma((uses, depth)),
            dma((uses, depth)),
            dma((uses, depth)),
            dma((uses,)),
            dma((uses,)),
            dma((uses, depth)),
            dma((uses, depth)),
            dma((uses, depth)),
            dma((uses, depth)),
        ],
        compiler_params=pltpu.CompilerParams(
            collective_id=0, has_side_effects=True, vmem_limit_bytes=60 << 20
        ),
    )(
        owners,
        entity.T,
        adagrad_state.reshape(1, rows),
        relation.T,
        source_ids,
        relation_ids,
        jnp.transpose(dest_groups, (0, 2, 1)),
        dest_rows,
        negative_ids,
    )
    return (table.T, state.reshape(rows))


def solution(mesh):
    placed = (
        P(("group", "member"), None),
        P(("group", "member")),
        P(),
        P(None, ("group", "member")),
        P(None, ("group", "member")),
        P(None, ("group", "member"), None),
        P(None, ("group", "member")),
        P(None, ("group", "member")),
        P(),
    )
    return jax.shard_map(
        functools.partial(per_device, mesh.shape["group"], mesh.shape["member"]),
        mesh=mesh,
        in_specs=placed,
        out_specs=(P(("group", "member"), None), P(("group", "member"))),
        check_vma=False,
    )
```

```python
import functools

import jax
import jax.numpy as jnp
from jax import lax
from jax.experimental import pallas as pl
from jax.experimental.pallas import tpu as pltpu
from jax.sharding import PartitionSpec as P

MESH = pl.DeviceIdType.MESH
F32 = jnp.float32
BF16 = jnp.bfloat16
LANES = 128
CAP = 128
LOW = -1e30


def dot_nn(a, b):
    return lax.dot_general(a, b, (((1,), (0,)), ((), ())), preferred_element_type=F32)


def dot_nt(a, b):
    return lax.dot_general(a, b, (((1,), (1,)), ((), ())), preferred_element_type=F32)


def dot_tn(a, b):
    return lax.dot_general(a, b, (((0,), (0,)), ((), ())), preferred_element_type=F32)


def iota(shape, dim):
    return lax.broadcasted_iota(jnp.int32, shape, dim)


def onehot(mask):
    return jnp.where(mask, 1.0, 0.0).astype(BF16)


def complex_parts(value, main):
    return value[:, :main], value[:, main : 2 * main], value[:, 2 * main :]


def tail_forms(tail, first):
    swapped = pltpu.roll(tail, LANES // 2, 1)
    return jnp.where(first, tail, swapped), jnp.where(first, swapped, tail)


def times(source, rel, main, first, sign):
    sr, si, st = complex_parts(source, main)
    rr, ri, rt = complex_parts(rel, main)
    tr, ti = tail_forms(rt, first)
    mixed = st * tr + sign * (pltpu.roll(st, LANES // 2, 1) * ti)
    return jnp.concatenate([sr * rr - si * ri, sr * ri + si * rr, mixed], 1)


def times_conjugate(grad, rel, main, first, sign):
    gr, gi, gt = complex_parts(grad, main)
    rr, ri, rt = complex_parts(rel, main)
    tr, ti = tail_forms(rt, first)
    mixed = gt * tr - sign * (pltpu.roll(gt, LANES // 2, 1) * ti)
    return jnp.concatenate([gr * rr + gi * ri, gi * rr - gr * ri, mixed], 1)


def pack(value, main, tail):
    count = value.shape[0]
    part = count // (LANES // 2 // tail)
    tiles = [value[:, c : c + LANES] for c in range(0, 2 * main, LANES)]
    last = value[:, 2 * main :]
    mixed = last[:part]
    for j in range(1, count // part):
        mixed = mixed + pltpu.roll(last[j * part : (j + 1) * part], tail * j, 1)
    return jnp.concatenate(tiles + [mixed], 0)


def unpack(stack, count, main, tail):
    part = count // (LANES // 2 // tail)
    tiles = 2 * main // LANES
    mixed = stack[tiles * count : tiles * count + part]
    used = iota((1, LANES), 1) % (LANES // 2) < tail
    last = [jnp.where(used, mixed, 0.0)]
    for j in range(1, count // part):
        last.append(jnp.where(used, pltpu.roll(mixed, LANES - tail * j, 1), 0.0))
    columns = [stack[c * count : (c + 1) * count] for c in range(tiles)]
    return jnp.concatenate(columns + [jnp.concatenate(last, 0)], 1)


def kernel(
    groups,
    members,
    owners,
    entity,
    state_in,
    relation,
    source_ids,
    relation_ids,
    dest_groups,
    dest_rows,
    negative_ids,
    entity_out,
    state_out,
    place,
    table,
    state,
    rel_table,
    edge_src,
    edge_rel,
    facts,
    taken,
    given,
    ids_send,
    ids_recv,
    counts,
    rel_edges,
    query,
    neg_exp,
    neg_max,
    neg_sum,
    weights,
    coef,
    dest,
    grad_dest,
    row_send,
    row_recv,
    grad_send,
    grad_recv,
    block,
    source_acc,
    grads,
    ar_in,
    ar_half,
    ar_mine,
    ar_parts,
    ar_piece,
    ar_other,
    ar_out,
    ids_ss,
    ids_rs,
    row_ss,
    row_rs,
    grad_ss,
    grad_rs,
    p1_ss,
    p1_rs,
    p2_ss,
    p2_rs,
    p3_ss,
    p3_rs,
    p4_ss,
    p4_rs,
    p5_ss,
    p5_rs,
):
    steps, edges = source_ids.shape
    width, rows = entity.shape
    rel_rows = relation.shape[1]
    half = width // 2
    main = half // LANES * LANES
    wide = table.shape[1]
    tail = half - main
    share = rows // 2
    piece = ar_half.shape[2]
    slots = groups * CAP
    depth = members // 4
    rings = groups // 2

    g = lax.axis_index("group")
    m = lax.axis_index("member")
    gx, gy = g // rings, g % rings
    core, z, xh = m % 2, (m // 2) % depth, m // (2 * depth)
    twin = m + 1 - 2 * core
    across = (m + 2 * depth) % members

    hops = [(0, j) for j in range(rings)]
    hops += sorted(((1, j) for j in range(rings)), key=lambda hop: -min(hop[1], rings - hop[1]))

    def peer(k):
        return ((gx + hops[k][0]) % 2) * rings + (gy + hops[k][1]) % rings

    def mirror(k):
        return hops.index((hops[k][0], -hops[k][1] % rings))

    def floor(k):
        return (z + k) % depth

    def along(other):
        return (g, xh * (2 * depth) + other * 2 + core)

    def remote(src, dst, send_sem, recv_sem, device):
        return pltpu.make_async_remote_copy(
            src_ref=src,
            dst_ref=dst,
            send_sem=send_sem,
            recv_sem=recv_sem,
            device_id=device,
            device_id_type=MESH,
        )

    barrier = pltpu.get_barrier_semaphore()

    for k in range(1, groups):
        pl.semaphore_signal(barrier, inc=1, device_id=(peer(k), m), device_id_type=MESH)
    for k in range(1, depth):
        pl.semaphore_signal(barrier, inc=1, device_id=along(floor(k)), device_id_type=MESH)
    pl.semaphore_signal(barrier, inc=1, device_id=(g, twin), device_id_type=MESH)
    pl.semaphore_signal(barrier, inc=1, device_id=(g, across), device_id_type=MESH)

    def ids_copy(s, k):
        return remote(
            ids_send.at[s, k],
            ids_recv.at[s, mirror(k)],
            ids_ss.at[s, k],
            ids_rs.at[s, mirror(k)],
            (peer(k), m),
        )

    def ids_arrival(s, k):
        return remote(
            ids_send.at[s, k], ids_recv.at[s, k], ids_ss.at[s, k], ids_rs.at[s, k], (peer(k), m)
        )

    def assign_slots(turns):
        before = onehot(iota((edges, edges), 0) < iota((edges, edges), 1))
        for s in turns:
            group_row = dest_groups[s]
            hop_x = (group_row // rings + 2 - gx) % 2
            hop_y = (group_row % rings + rings - gy) % rings
            where = hop_x * rings + hop_y
            hop = jnp.zeros_like(where)
            for k in range(groups):
                hop = jnp.where(where == hops[k][0] * rings + hops[k][1], k, hop)
            named = iota((16, edges), 0) == hop
            rank = dot_nn(onehot(named), before)
            rank = jnp.sum(jnp.where(named, rank, 0.0), 0, keepdims=True).astype(jnp.int32)
            taken[s] = onehot(iota((slots, edges), 0) == hop * CAP + rank)
            rel_row = relation_ids[s : s + 1, :]
            high = rel_row // 32
            which = iota((16, edges), 0)
            known = jnp.where(which == 0, source_ids[s : s + 1, :], 0)
            known = jnp.where(which == 1, high, known)
            known = jnp.where(which == 2, rel_row - 32 * high, known)
            known = jnp.where(which == 3, dest_rows[s : s + 1, :], known)
            known = jnp.where(which == 4, 1, known)
            known = jnp.where(which == 5, hop, known)
            known = jnp.where(which == 6, rank, known)
            facts[s] = known.astype(F32).astype(BF16)
            flat = dot_nt(facts[s], taken[s]).astype(jnp.int32)
            wanted = flat[3:4, :] + 4 * rows * (flat[4:5, :] - 1)
            for k in range(groups):
                ids_send[s, k] = jnp.broadcast_to(wanted[:, k * CAP : (k + 1) * CAP], (8, CAP))

    def ids_start(turns):
        for s in turns:
            for k in range(1, groups):
                ids_copy(s, k).start()
            ids_recv[s, 0] = ids_send[s, 0]

    assign_slots(range(1))
    pl.semaphore_wait(barrier, groups + depth)
    ids_start(range(1))

    comp = iota((width, 1), 0)
    imag = comp >= half
    local = jnp.where(imag, comp - half, comp)
    spot = jnp.where(
        local < main,
        local + jnp.where(imag, main, 0),
        2 * main + jnp.where(imag, LANES // 2, 0) + local - main,
    )
    place[...] = onehot(iota((width, wide), 1) == spot)
    table[...] = dot_tn(entity[...], place[...]).astype(BF16)
    eye = iota((rows, rows), 0) == iota((rows, rows), 1)
    state[...] = jnp.sum(jnp.where(eye, state_in[...], 0.0), 1, keepdims=True)
    first = iota((1, LANES), 1) < LANES // 2
    sign = jnp.where(first, -1.0, 1.0)

    def edge_columns():
        same = onehot(iota((edges, edges), 0) == iota((edges, edges), 1))
        for s in range(steps):
            tall = dot_nt(same, facts[s]).astype(jnp.int32)
            edge_src[s] = tall[:, 0:1]
            edge_rel[s] = 32 * tall[:, 1:2] + tall[:, 2:3]
            given[s] = onehot(iota((edges, slots), 1) == CAP * tall[:, 5:6] + tall[:, 6:7])

    def ids_wait(turns):
        for s in turns:
            for k in range(1, groups):
                ids_copy(s, k).wait_send()
                ids_arrival(s, k).wait_recv()

    near = sorted(range(1, depth), key=lambda k: min(k, depth - k))
    far = near[::-1]

    def ar_fill(i, value):
        for h in range(2):
            stack = pack(value[h * share : (h + 1) * share], main, tail)
            spare = jnp.zeros((depth * piece - stack.shape[0], LANES), F32)
            stack = jnp.concatenate([stack, spare], 0)
            ar_in[i, h] = stack.reshape(depth, piece, LANES).astype(BF16)

    def ar_read(i):
        halves = []
        for h in range(2):
            stack = ar_out[i, h].astype(F32).reshape(depth * piece, LANES)
            halves.append(unpack(stack, share, main, tail))
        return jnp.concatenate(halves, 0)

    def ar_first_copy(i, other):
        return remote(
            ar_in.at[i, 1 - core, other],
            ar_half.at[i, other],
            p1_ss.at[i, other],
            p1_rs.at[i, other],
            (g, twin),
        )

    def ar_first(i):
        for k in far + [0]:
            ar_first_copy(i, floor(k)).start()

    def ar_scatter_copy(i, other):
        return remote(
            ar_mine.at[i, other],
            ar_parts.at[i, z],
            p2_ss.at[i, other],
            p2_rs.at[i, z],
            along(other),
        )

    def ar_scatter_arrival(i, other):
        return remote(
            ar_mine.at[i, other],
            ar_parts.at[i, other],
            p2_ss.at[i, other],
            p2_rs.at[i, other],
            along(other),
        )

    def ar_cross_copy(i):
        return remote(ar_piece.at[i], ar_other.at[i], p3_ss.at[i], p3_rs.at[i], (g, across))

    def ar_gather_copy(i, other):
        return remote(
            ar_out.at[i, core, z],
            ar_out.at[i, core, z],
            p4_ss.at[i, other],
            p4_rs.at[i, z],
            along(other),
        )

    def ar_gather_arrival(i, other):
        return remote(
            ar_out.at[i, core, other],
            ar_out.at[i, core, other],
            p4_ss.at[i, other],
            p4_rs.at[i, other],
            along(other),
        )

    def ar_last(i, which, other):
        return remote(
            ar_out.at[i, which, other],
            ar_out.at[i, which, other],
            p5_ss.at[i, other],
            p5_rs.at[i, other],
            (g, twin),
        )

    def ar_scatter(i):
        for k in far + [0]:
            other = floor(k)
            ar_first_copy(i, other).wait()
            mine = ar_in[i, core, other].astype(F32) + ar_half[i, other].astype(F32)
            ar_mine[i, other] = mine.astype(BF16)
            if k:
                ar_scatter_copy(i, other).start()

    def ar_cross(i):
        @pl.loop(1, depth)
        def _(k):
            other = floor(k)
            ar_scatter_copy(i, other).wait_send()
            ar_scatter_arrival(i, other).wait_recv()

        ar_parts[i, z] = ar_mine[i, z]
        piece = jnp.sum(ar_parts[i].astype(F32), 0)
        ar_piece[i] = piece.astype(BF16)
        ar_cross_copy(i).start()

    def ar_gather(i):
        ar_cross_copy(i).wait()
        whole = ar_piece[i].astype(F32) + ar_other[i].astype(F32)
        ar_out[i, core, z] = whole.astype(BF16)
        for k in far:
            ar_gather_copy(i, floor(k)).start()
        ar_last(i, core, z).start()

    def ar_share(i):
        for k in near:
            other = floor(k)
            ar_gather_arrival(i, other).wait_recv()
            ar_last(i, core, other).start()

    def ar_done(i):
        for k in [0] + near:
            other = floor(k)
            if k:
                ar_gather_copy(i, other).wait_send()
            ar_last(i, core, other).wait_send()
            ar_last(i, 1 - core, other).wait_recv()

    @pl.loop(0, steps)
    def _(s):
        root = owners[s, g]
        fetch, reduce = 2 * s, 2 * s + 1

        def row_copy(k):
            return remote(
                row_send.at[s, k],
                row_recv.at[s, mirror(k)],
                row_ss.at[s, k],
                row_rs.at[s, mirror(k)],
                (peer(k), m),
            )

        def row_arrival(k):
            return remote(
                row_send.at[s, k], row_recv.at[s, k], row_ss.at[s, k], row_rs.at[s, k], (peer(k), m)
            )

        def grad_copy(k):
            return remote(
                grad_send.at[s, k],
                grad_recv.at[s, mirror(k)],
                grad_ss.at[s, k],
                grad_rs.at[s, mirror(k)],
                (peer(k), m),
            )

        def grad_arrival(k):
            return remote(
                grad_send.at[s, k],
                grad_recv.at[s, k],
                grad_ss.at[s, k],
                grad_rs.at[s, k],
                (peer(k), m),
            )

        def asked(p):
            ids = [ids_recv[s, 2 * p + j, 0:1, :] for j in range(2)]
            return onehot(iota((rows, 2 * CAP), 0) == jnp.concatenate(ids, 1))

        def pick_rows(p):
            picked = dot_tn(asked(p), table[...])
            for j in range(2):
                row_send[s, 2 * p + j] = pack(picked[j * CAP : (j + 1) * CAP], main, tail).astype(BF16)

        def send_rows(p):
            for k in (2 * p, 2 * p + 1):
                if k:
                    row_copy(k).start()

        def relations(k):
            here = pl.ds(pl.multiple_of(k * 2 * CAP, 2 * CAP), 2 * CAP)
            chosen = onehot(iota((2 * CAP, rel_rows), 1) == edge_rel[s, here, :])
            rel_edges[here, :] = dot_nn(chosen, rel_table[...]).astype(BF16)

        def collect(p):
            for k in (2 * p, 2 * p + 1):
                if k:
                    row_copy(k).wait_send()
                    row_arrival(k).wait_recv()
            arrived = [unpack(row_recv[s, k].astype(F32), CAP, main, tail) for k in (2 * p, 2 * p + 1)]
            arrived = jnp.concatenate(arrived, 0).astype(BF16)
            sorted_rows = dot_nn(given[s, :, 2 * p * CAP : (2 * p + 2) * CAP], arrived)
            dest[...] = sorted_rows if p == 0 else dest[...] + sorted_rows

        def make_grads(p):
            block_rows = taken[s, 2 * p * CAP : (2 * p + 2) * CAP, :]
            spread = dot_nn(block_rows, grad_dest[...])
            for j in range(2):
                stack = pack(spread[j * CAP : (j + 1) * CAP], main, tail)
                grad_send[s, 2 * p + j] = stack.astype(BF16)

        def send_grads(p):
            for k in (2 * p, 2 * p + 1):
                if k:
                    grad_copy(k).start()

        @pl.when(s > 0)
        def _():
            pick_rows(2)
            send_rows(2)

        ar_fill(fetch, jnp.where(m == root, table[...].astype(F32), 0.0))
        ar_first(fetch)
        ar_scatter(fetch)

        @pl.when(s == 0)
        def _():
            ids_wait(range(1))
            pick_rows(2)
            row_copy(4).start()

        pick_rows(0)
        send_rows(0)
        row_recv[s, 0] = row_send[s, 0]
        pick_rows(1)
        send_rows(1)
        pick_rows(3)

        @pl.when(s == 0)
        def _():
            assign_slots(range(1, steps))
            ids_start(range(1, steps))
            edge_columns()
            rel_table[...] = dot_tn(relation[...], place[...]).astype(BF16)

        slot_count = negative_ids.shape[1]
        hits = onehot(iota((rows, slot_count), 0) == negative_ids[pl.ds(s, 1), :])
        counts[...] = dot_nt(jnp.ones((8, slot_count), BF16), hits)
        ar_cross(fetch)

        @pl.when(s == 0)
        def _():
            row_copy(5).start()

        send_rows(3)

        relations(0)
        ar_gather(fetch)
        relations(1)
        ar_share(fetch)
        source_acc[...] = jnp.zeros_like(source_acc)
        count_row = counts[0:1, :]
        present = count_row > 0.5
        ar_done(fetch)
        block[...] = ar_read(fetch).astype(BF16)

        @pl.loop(0, edges // (2 * CAP))
        def _(k):
            here = pl.ds(pl.multiple_of(k * 2 * CAP, 2 * CAP), 2 * CAP)
            chosen = onehot(iota((2 * CAP, rows), 1) == edge_src[s, here, :])
            source = dot_nn(chosen, block[...])
            q = times(source, rel_edges[here, :].astype(F32), main, first, sign).astype(BF16)
            query[here, :] = q
            scores = jnp.where(present, dot_nt(q, table[...]), LOW)
            top = jnp.max(scores, 1, keepdims=True)
            e = jnp.exp(scores - top) * count_row
            neg_exp[here, :] = e
            neg_max[here, :] = top
            neg_sum[here, :] = jnp.sum(e, 1, keepdims=True)

        collect(0)
        collect(1)
        collect(2)
        collect(3)

        @pl.loop(0, edges // (2 * CAP))
        def _(k):
            here = pl.ds(pl.multiple_of(k * 2 * CAP, 2 * CAP), 2 * CAP)
            q = query[here, :].astype(F32)
            positive = jnp.sum(q * dest[here, :], 1, keepdims=True)
            low = neg_max[here, :]
            top = jnp.maximum(low, positive)
            pos_exp = jnp.exp(positive - top)
            shrink = jnp.exp(low - top)
            total = pos_exp + neg_sum[here, :] * shrink
            coef_pos = pos_exp / total - 1.0
            coef[here, :] = coef_pos
            grad_dest[here, :] = (coef_pos * q).astype(BF16)
            weights[here, :] = (neg_exp[here, :] * (shrink / total)).astype(BF16)

        make_grads(2)
        send_grads(2)

        @pl.loop(0, edges // (2 * CAP))
        def _(k):
            base = pl.multiple_of(k * 2 * CAP, 2 * CAP)
            here = pl.ds(base, 2 * CAP)
            grad_query = coef[here, :] * dest[here, :] + dot_nn(weights[here, :], table[...])
            grad_source = times_conjugate(
                grad_query, rel_edges[here, :].astype(F32), main, first, sign
            ).astype(BF16)
            spread = onehot(iota((rows, 2 * CAP), 0) == source_ids[pl.ds(s, 1), here])
            source_acc[...] += dot_nn(spread, grad_source)

        ar_fill(reduce, source_acc[...])
        ar_first(reduce)
        make_grads(0)
        send_grads(0)
        grad_recv[s, 0] = grad_send[s, 0]
        ar_scatter(reduce)
        make_grads(1)
        send_grads(1)
        make_grads(3)
        grads[...] = dot_tn(weights[...], query[...])
        ar_cross(reduce)
        send_grads(3)
        ar_gather(reduce)

        def scatter_grads(p):
            for k in (2 * p, 2 * p + 1):
                if k:
                    grad_copy(k).wait_send()
                    grad_arrival(k).wait_recv()
            arrived = [unpack(grad_recv[s, k].astype(F32), CAP, main, tail) for k in (2 * p, 2 * p + 1)]
            grads[...] += dot_nn(asked(p), jnp.concatenate(arrived, 0).astype(BF16))

        scatter_grads(2)
        scatter_grads(0)
        scatter_grads(1)
        ar_share(reduce)
        scatter_grads(3)
        ar_done(reduce)

        @pl.when(s == 0)
        def _():
            ids_wait(range(1, steps))

        total = grads[...] + jnp.where(m == root, ar_read(reduce), 0.0)
        fresh = state[...] + jnp.sum(total * total, 1, keepdims=True) * (1.0 / width)
        state[...] = fresh
        table[...] = (table[...].astype(F32) - total / jnp.sqrt(fresh)).astype(BF16)

    entity_out[...] = dot_nt(place[...], table[...]).astype(BF16)
    state_out[...] = jnp.sum(jnp.where(eye, state[...], 0.0), 0, keepdims=True)


def per_device(
    groups,
    members,
    entity,
    adagrad_state,
    relation,
    source_ids,
    relation_ids,
    dest_groups,
    dest_rows,
    negative_ids,
    owners,
):
    rows, width = entity.shape
    steps, edges = source_ids.shape
    half = width // 2
    wide = 2 * (half // LANES * LANES) + LANES
    slots = groups * CAP
    depth = members // 4
    stack = CAP * width // LANES
    piece = -(-rows // 2 * width // LANES // depth // 8) * 8
    uses = 2 * steps
    dma = pltpu.SemaphoreType.DMA
    vmem = pltpu.VMEM
    whole = pl.BlockSpec(memory_space=pltpu.VMEM)
    table, state = pl.pallas_call(
        functools.partial(kernel, groups, members),
        out_shape=(
            jax.ShapeDtypeStruct((width, rows), BF16),
            jax.ShapeDtypeStruct((1, rows), F32),
        ),
        in_specs=[pl.BlockSpec(memory_space=pltpu.SMEM)] + [whole] * 8,
        out_specs=(whole, whole),
        scratch_shapes=[
            vmem((width, wide), BF16),
            vmem((rows, wide), BF16),
            vmem((rows, 1), F32),
            vmem((relation.shape[0], wide), BF16),
            vmem((steps, edges, 1), jnp.int32),
            vmem((steps, edges, 1), jnp.int32),
            vmem((steps, 16, edges), BF16),
            vmem((steps, slots, edges), BF16),
            vmem((steps, edges, slots), BF16),
            vmem((steps, groups, 8, CAP), jnp.int32),
            vmem((steps, groups, 8, CAP), jnp.int32),
            vmem((8, rows), F32),
            vmem((edges, wide), BF16),
            vmem((edges, wide), BF16),
            vmem((edges, rows), F32),
            vmem((edges, 1), F32),
            vmem((edges, 1), F32),
            vmem((edges, rows), BF16),
            vmem((edges, 1), F32),
            vmem((edges, wide), F32),
            vmem((edges, wide), BF16),
            vmem((steps, groups, stack, LANES), BF16),
            vmem((steps, groups, stack, LANES), BF16),
            vmem((steps, groups, stack, LANES), BF16),
            vmem((steps, groups, stack, LANES), BF16),
            vmem((rows, wide), BF16),
            vmem((rows, wide), F32),
            vmem((rows, wide), F32),
            vmem((uses, 2, depth, piece, LANES), BF16),
            vmem((uses, depth, piece, LANES), BF16),
            vmem((uses, depth, piece, LANES), BF16),
            vmem((uses, depth, piece, LANES), BF16),
            vmem((uses, piece, LANES), BF16),
            vmem((uses, piece, LANES), BF16),
            vmem((uses, 2, depth, piece, LANES), BF16),
            dma((steps, groups)),
            dma((steps, groups)),
            dma((steps, groups)),
            dma((steps, groups)),
            dma((steps, groups)),
            dma((steps, groups)),
            dma((uses, depth)),
            dma((uses, depth)),
            dma((uses, depth)),
            dma((uses, depth)),
            dma((uses,)),
            dma((uses,)),
            dma((uses, depth)),
            dma((uses, depth)),
            dma((uses, depth)),
            dma((uses, depth)),
        ],
        compiler_params=pltpu.CompilerParams(
            collective_id=0, has_side_effects=True, vmem_limit_bytes=60 << 20
        ),
    )(
        owners,
        entity.T,
        adagrad_state.reshape(1, rows),
        relation.T,
        source_ids,
        relation_ids,
        jnp.transpose(dest_groups, (0, 2, 1)),
        dest_rows,
        negative_ids,
    )
    return (table.T, state.reshape(rows))


def solution(mesh):
    placed = (
        P(("group", "member"), None),
        P(("group", "member")),
        P(),
        P(None, ("group", "member")),
        P(None, ("group", "member")),
        P(None, ("group", "member"), None),
        P(None, ("group", "member")),
        P(None, ("group", "member")),
        P(),
    )
    return jax.shard_map(
        functools.partial(per_device, mesh.shape["group"], mesh.shape["member"]),
        mesh=mesh,
        in_specs=placed,
        out_specs=(P(("group", "member"), None), P(("group", "member"))),
        check_vma=False,
    )
```

```python
import functools

import jax
import jax.numpy as jnp
from jax import lax
from jax.experimental import pallas as pl
from jax.experimental.pallas import tpu as pltpu
from jax.sharding import PartitionSpec as P

MESH = pl.DeviceIdType.MESH
F32 = jnp.float32
BF16 = jnp.bfloat16
LANES = 128
CAP = 128
LOW = -1e30


def dot_nn(a, b):
    return lax.dot_general(a, b, (((1,), (0,)), ((), ())), preferred_element_type=F32)


def dot_nt(a, b):
    return lax.dot_general(a, b, (((1,), (1,)), ((), ())), preferred_element_type=F32)


def dot_tn(a, b):
    return lax.dot_general(a, b, (((0,), (0,)), ((), ())), preferred_element_type=F32)


def iota(shape, dim):
    return lax.broadcasted_iota(jnp.int32, shape, dim)


def onehot(mask):
    return jnp.where(mask, 1.0, 0.0).astype(BF16)


def complex_parts(value, main):
    return value[:, :main], value[:, main : 2 * main], value[:, 2 * main :]


def tail_forms(tail, first):
    swapped = pltpu.roll(tail, LANES // 2, 1)
    return jnp.where(first, tail, swapped), jnp.where(first, swapped, tail)


def times(source, rel, main, first, sign):
    sr, si, st = complex_parts(source, main)
    rr, ri, rt = complex_parts(rel, main)
    tr, ti = tail_forms(rt, first)
    mixed = st * tr + sign * (pltpu.roll(st, LANES // 2, 1) * ti)
    return jnp.concatenate([sr * rr - si * ri, sr * ri + si * rr, mixed], 1)


def times_conjugate(grad, rel, main, first, sign):
    gr, gi, gt = complex_parts(grad, main)
    rr, ri, rt = complex_parts(rel, main)
    tr, ti = tail_forms(rt, first)
    mixed = gt * tr - sign * (pltpu.roll(gt, LANES // 2, 1) * ti)
    return jnp.concatenate([gr * rr + gi * ri, gi * rr - gr * ri, mixed], 1)


def pack(value, main, tail):
    count = value.shape[0]
    part = count // (LANES // 2 // tail)
    tiles = [value[:, c : c + LANES] for c in range(0, 2 * main, LANES)]
    last = value[:, 2 * main :]
    mixed = last[:part]
    for j in range(1, count // part):
        mixed = mixed + pltpu.roll(last[j * part : (j + 1) * part], tail * j, 1)
    return jnp.concatenate(tiles + [mixed], 0)


def unpack(stack, count, main, tail):
    part = count // (LANES // 2 // tail)
    tiles = 2 * main // LANES
    mixed = stack[tiles * count : tiles * count + part]
    used = iota((1, LANES), 1) % (LANES // 2) < tail
    last = [jnp.where(used, mixed, 0.0)]
    for j in range(1, count // part):
        last.append(jnp.where(used, pltpu.roll(mixed, LANES - tail * j, 1), 0.0))
    columns = [stack[c * count : (c + 1) * count] for c in range(tiles)]
    return jnp.concatenate(columns + [jnp.concatenate(last, 0)], 1)


def kernel(
    groups,
    members,
    owners,
    entity,
    state_in,
    relation,
    source_ids,
    relation_ids,
    dest_groups,
    dest_rows,
    negative_ids,
    entity_out,
    state_out,
    place,
    table,
    state,
    rel_raw,
    rel_sem,
    rel_table,
    edge_src,
    edge_rel,
    facts,
    taken,
    given,
    ids_send,
    ids_recv,
    counts,
    rel_edges,
    query,
    neg_exp,
    neg_max,
    neg_sum,
    weights,
    coef,
    dest,
    grad_dest,
    row_send,
    row_recv,
    grad_send,
    grad_recv,
    block,
    source_acc,
    grads,
    ar_in,
    ar_half,
    ar_mine,
    ar_parts,
    ar_piece,
    ar_other,
    ar_out,
    ids_ss,
    ids_rs,
    row_ss,
    row_rs,
    grad_ss,
    grad_rs,
    p1_ss,
    p1_rs,
    p2_ss,
    p2_rs,
    p3_ss,
    p3_rs,
    p4_ss,
    p4_rs,
    p5_ss,
    p5_rs,
):
    steps, edges = source_ids.shape
    width, rows = entity.shape
    rel_rows = relation.shape[1]
    half = width // 2
    main = half // LANES * LANES
    wide = table.shape[1]
    tail = half - main
    share = rows // 2
    piece = ar_half.shape[2]
    slots = groups * CAP
    depth = members // 4
    rings = groups // 2

    g = lax.axis_index("group")
    m = lax.axis_index("member")
    gx, gy = g // rings, g % rings
    core, z, xh = m % 2, (m // 2) % depth, m // (2 * depth)
    twin = m + 1 - 2 * core
    across = (m + 2 * depth) % members

    hops = [(0, j) for j in range(rings)]
    hops += sorted(((1, j) for j in range(rings)), key=lambda hop: -min(hop[1], rings - hop[1]))

    def peer(k):
        return ((gx + hops[k][0]) % 2) * rings + (gy + hops[k][1]) % rings

    def mirror(k):
        return hops.index((hops[k][0], -hops[k][1] % rings))

    def floor(k):
        return (z + k) % depth

    def along(other):
        return (g, xh * (2 * depth) + other * 2 + core)

    def remote(src, dst, send_sem, recv_sem, device):
        return pltpu.make_async_remote_copy(
            src_ref=src,
            dst_ref=dst,
            send_sem=send_sem,
            recv_sem=recv_sem,
            device_id=device,
            device_id_type=MESH,
        )

    barrier = pltpu.get_barrier_semaphore()
    fetch_relation = pltpu.make_async_copy(relation, rel_raw, rel_sem)
    fetch_relation.start()

    for k in range(1, groups):
        pl.semaphore_signal(barrier, inc=1, device_id=(peer(k), m), device_id_type=MESH)
    for k in range(1, depth):
        pl.semaphore_signal(barrier, inc=1, device_id=along(floor(k)), device_id_type=MESH)
    pl.semaphore_signal(barrier, inc=1, device_id=(g, twin), device_id_type=MESH)
    pl.semaphore_signal(barrier, inc=1, device_id=(g, across), device_id_type=MESH)

    def ids_copy(s, k):
        return remote(
            ids_send.at[s, k],
            ids_recv.at[s, mirror(k)],
            ids_ss.at[s, k],
            ids_rs.at[s, mirror(k)],
            (peer(k), m),
        )

    def ids_arrival(s, k):
        return remote(
            ids_send.at[s, k], ids_recv.at[s, k], ids_ss.at[s, k], ids_rs.at[s, k], (peer(k), m)
        )

    def assign_slots(turns):
        before = onehot(iota((edges, edges), 0) < iota((edges, edges), 1))
        for s in turns:
            group_row = dest_groups[s]
            hop_x = (group_row // rings + 2 - gx) % 2
            hop_y = (group_row % rings + rings - gy) % rings
            where = hop_x * rings + hop_y
            hop = jnp.zeros_like(where)
            for k in range(groups):
                hop = jnp.where(where == hops[k][0] * rings + hops[k][1], k, hop)
            named = iota((16, edges), 0) == hop
            rank = dot_nn(onehot(named), before)
            rank = jnp.sum(jnp.where(named, rank, 0.0), 0, keepdims=True).astype(jnp.int32)
            taken[s] = onehot(iota((slots, edges), 0) == hop * CAP + rank)
            rel_row = relation_ids[s : s + 1, :]
            high = rel_row // 32
            which = iota((16, edges), 0)
            known = jnp.where(which == 0, source_ids[s : s + 1, :], 0)
            known = jnp.where(which == 1, high, known)
            known = jnp.where(which == 2, rel_row - 32 * high, known)
            known = jnp.where(which == 3, dest_rows[s : s + 1, :], known)
            known = jnp.where(which == 4, 1, known)
            known = jnp.where(which == 5, hop, known)
            known = jnp.where(which == 6, rank, known)
            facts[s] = known.astype(F32).astype(BF16)
            flat = dot_nt(facts[s], taken[s]).astype(jnp.int32)
            wanted = flat[3:4, :] + 4 * rows * (flat[4:5, :] - 1)
            for k in range(groups):
                ids_send[s, k] = jnp.broadcast_to(wanted[:, k * CAP : (k + 1) * CAP], (8, CAP))

    def ids_start(turns):
        for s in turns:
            for k in range(1, groups):
                ids_copy(s, k).start()
            ids_recv[s, 0] = ids_send[s, 0]

    assign_slots(range(1))
    pl.semaphore_wait(barrier, groups + depth)
    ids_start(range(1))

    comp = iota((width, 1), 0)
    imag = comp >= half
    local = jnp.where(imag, comp - half, comp)
    spot = jnp.where(
        local < main,
        local + jnp.where(imag, main, 0),
        2 * main + jnp.where(imag, LANES // 2, 0) + local - main,
    )
    place[...] = onehot(iota((width, wide), 1) == spot)
    table[...] = dot_tn(entity[...], place[...]).astype(BF16)
    eye = iota((rows, rows), 0) == iota((rows, rows), 1)
    state[...] = jnp.sum(jnp.where(eye, state_in[...], 0.0), 1, keepdims=True)
    first = iota((1, LANES), 1) < LANES // 2
    sign = jnp.where(first, -1.0, 1.0)

    def edge_columns():
        same = onehot(iota((edges, edges), 0) == iota((edges, edges), 1))
        for s in range(steps):
            tall = dot_nt(same, facts[s]).astype(jnp.int32)
            edge_src[s] = tall[:, 0:1]
            edge_rel[s] = 32 * tall[:, 1:2] + tall[:, 2:3]
            given[s] = onehot(iota((edges, slots), 1) == CAP * tall[:, 5:6] + tall[:, 6:7])

    def ids_wait(turns):
        for s in turns:
            for k in range(1, groups):
                ids_copy(s, k).wait_send()
                ids_arrival(s, k).wait_recv()

    near = sorted(range(1, depth), key=lambda k: min(k, depth - k))
    far = near[::-1]

    def ar_fill(i, value):
        for h in range(2):
            stack = pack(value[h * share : (h + 1) * share], main, tail)
            spare = jnp.zeros((depth * piece - stack.shape[0], LANES), F32)
            stack = jnp.concatenate([stack, spare], 0)
            ar_in[i, h] = stack.reshape(depth, piece, LANES).astype(BF16)

    def ar_read(i):
        halves = []
        for h in range(2):
            stack = ar_out[i, h].astype(F32).reshape(depth * piece, LANES)
            halves.append(unpack(stack, share, main, tail))
        return jnp.concatenate(halves, 0)

    def ar_first_copy(i, other):
        return remote(
            ar_in.at[i, 1 - core, other],
            ar_half.at[i, other],
            p1_ss.at[i, other],
            p1_rs.at[i, other],
            (g, twin),
        )

    def ar_first(i):
        for k in far + [0]:
            ar_first_copy(i, floor(k)).start()

    def ar_scatter_copy(i, other):
        return remote(
            ar_mine.at[i, other],
            ar_parts.at[i, z],
            p2_ss.at[i, other],
            p2_rs.at[i, z],
            along(other),
        )

    def ar_scatter_arrival(i, other):
        return remote(
            ar_mine.at[i, other],
            ar_parts.at[i, other],
            p2_ss.at[i, other],
            p2_rs.at[i, other],
            along(other),
        )

    def ar_cross_copy(i):
        return remote(ar_piece.at[i], ar_other.at[i], p3_ss.at[i], p3_rs.at[i], (g, across))

    def ar_gather_copy(i, other):
        return remote(
            ar_out.at[i, core, z],
            ar_out.at[i, core, z],
            p4_ss.at[i, other],
            p4_rs.at[i, z],
            along(other),
        )

    def ar_gather_arrival(i, other):
        return remote(
            ar_out.at[i, core, other],
            ar_out.at[i, core, other],
            p4_ss.at[i, other],
            p4_rs.at[i, other],
            along(other),
        )

    def ar_last(i, which, other):
        return remote(
            ar_out.at[i, which, other],
            ar_out.at[i, which, other],
            p5_ss.at[i, other],
            p5_rs.at[i, other],
            (g, twin),
        )

    def ar_scatter(i):
        for k in far + [0]:
            other = floor(k)
            ar_first_copy(i, other).wait()
            mine = ar_in[i, core, other].astype(F32) + ar_half[i, other].astype(F32)
            ar_mine[i, other] = mine.astype(BF16)
            if k:
                ar_scatter_copy(i, other).start()

    def ar_cross(i):
        @pl.loop(1, depth)
        def _(k):
            other = floor(k)
            ar_scatter_copy(i, other).wait_send()
            ar_scatter_arrival(i, other).wait_recv()

        ar_parts[i, z] = ar_mine[i, z]
        piece = jnp.sum(ar_parts[i].astype(F32), 0)
        ar_piece[i] = piece.astype(BF16)
        ar_cross_copy(i).start()

    def ar_gather(i):
        ar_cross_copy(i).wait()
        whole = ar_piece[i].astype(F32) + ar_other[i].astype(F32)
        ar_out[i, core, z] = whole.astype(BF16)
        for k in far:
            ar_gather_copy(i, floor(k)).start()
        ar_last(i, core, z).start()

    def ar_share(i):
        for k in near:
            other = floor(k)
            ar_gather_arrival(i, other).wait_recv()
            ar_last(i, core, other).start()

    def ar_done(i):
        for k in [0] + near:
            other = floor(k)
            if k:
                ar_gather_copy(i, other).wait_send()
            ar_last(i, core, other).wait_send()
            ar_last(i, 1 - core, other).wait_recv()

    @pl.loop(0, steps)
    def _(s):
        root = owners[s, g]
        fetch, reduce = 2 * s, 2 * s + 1

        def row_copy(k):
            return remote(
                row_send.at[s, k],
                row_recv.at[s, mirror(k)],
                row_ss.at[s, k],
                row_rs.at[s, mirror(k)],
                (peer(k), m),
            )

        def row_arrival(k):
            return remote(
                row_send.at[s, k], row_recv.at[s, k], row_ss.at[s, k], row_rs.at[s, k], (peer(k), m)
            )

        def grad_copy(k):
            return remote(
                grad_send.at[s, k],
                grad_recv.at[s, mirror(k)],
                grad_ss.at[s, k],
                grad_rs.at[s, mirror(k)],
                (peer(k), m),
            )

        def grad_arrival(k):
            return remote(
                grad_send.at[s, k],
                grad_recv.at[s, k],
                grad_ss.at[s, k],
                grad_rs.at[s, k],
                (peer(k), m),
            )

        def asked(p):
            ids = [ids_recv[s, 2 * p + j, 0:1, :] for j in range(2)]
            return onehot(iota((rows, 2 * CAP), 0) == jnp.concatenate(ids, 1))

        def pick_rows(p):
            picked = dot_tn(asked(p), table[...])
            for j in range(2):
                row_send[s, 2 * p + j] = pack(picked[j * CAP : (j + 1) * CAP], main, tail).astype(BF16)

        def send_rows(p):
            for k in (2 * p, 2 * p + 1):
                if k:
                    row_copy(k).start()

        def relations(k):
            here = pl.ds(pl.multiple_of(k * 2 * CAP, 2 * CAP), 2 * CAP)
            chosen = onehot(iota((2 * CAP, rel_rows), 1) == edge_rel[s, here, :])
            rel_edges[here, :] = dot_nn(chosen, rel_table[...]).astype(BF16)

        def collect(p):
            for k in (2 * p, 2 * p + 1):
                if k:
                    row_copy(k).wait_send()
                    row_arrival(k).wait_recv()
            arrived = [unpack(row_recv[s, k].astype(F32), CAP, main, tail) for k in (2 * p, 2 * p + 1)]
            arrived = jnp.concatenate(arrived, 0).astype(BF16)
            sorted_rows = dot_nn(given[s, :, 2 * p * CAP : (2 * p + 2) * CAP], arrived)
            dest[...] = sorted_rows if p == 0 else dest[...] + sorted_rows

        def make_grads(p):
            block_rows = taken[s, 2 * p * CAP : (2 * p + 2) * CAP, :]
            spread = dot_nn(block_rows, grad_dest[...])
            for j in range(2):
                stack = pack(spread[j * CAP : (j + 1) * CAP], main, tail)
                grad_send[s, 2 * p + j] = stack.astype(BF16)

        def send_grads(p):
            for k in (2 * p, 2 * p + 1):
                if k:
                    grad_copy(k).start()

        @pl.when(s > 0)
        def _():
            pick_rows(2)
            send_rows(2)

        ar_fill(fetch, jnp.where(m == root, table[...].astype(F32), 0.0))
        ar_first(fetch)
        ar_scatter(fetch)

        @pl.when(s == 0)
        def _():
            ids_wait(range(1))
            pick_rows(2)
            row_copy(4).start()

        pick_rows(0)
        send_rows(0)
        row_recv[s, 0] = row_send[s, 0]
        pick_rows(1)
        send_rows(1)
        pick_rows(3)

        @pl.when(s == 0)
        def _():
            assign_slots(range(1, steps))
            ids_start(range(1, steps))
            edge_columns()
            fetch_relation.wait()
            rel_table[...] = dot_tn(rel_raw[...], place[...]).astype(BF16)

        slot_count = negative_ids.shape[1]
        hits = onehot(iota((rows, slot_count), 0) == negative_ids[pl.ds(s, 1), :])
        counts[...] = dot_nt(jnp.ones((8, slot_count), BF16), hits)
        ar_cross(fetch)

        @pl.when(s == 0)
        def _():
            row_copy(5).start()

        send_rows(3)

        relations(0)
        ar_gather(fetch)
        relations(1)
        ar_share(fetch)
        source_acc[...] = jnp.zeros_like(source_acc)
        count_row = counts[0:1, :]
        present = count_row > 0.5
        ar_done(fetch)
        block[...] = ar_read(fetch).astype(BF16)

        @pl.loop(0, edges // (2 * CAP))
        def _(k):
            here = pl.ds(pl.multiple_of(k * 2 * CAP, 2 * CAP), 2 * CAP)
            chosen = onehot(iota((2 * CAP, rows), 1) == edge_src[s, here, :])
            source = dot_nn(chosen, block[...])
            q = times(source, rel_edges[here, :].astype(F32), main, first, sign).astype(BF16)
            query[here, :] = q
            scores = jnp.where(present, dot_nt(q, table[...]), LOW)
            top = jnp.max(scores, 1, keepdims=True)
            e = jnp.exp(scores - top) * count_row
            neg_exp[here, :] = e
            neg_max[here, :] = top
            neg_sum[here, :] = jnp.sum(e, 1, keepdims=True)

        collect(0)
        collect(1)
        collect(2)
        collect(3)

        @pl.loop(0, edges // (2 * CAP))
        def _(k):
            here = pl.ds(pl.multiple_of(k * 2 * CAP, 2 * CAP), 2 * CAP)
            q = query[here, :].astype(F32)
            positive = jnp.sum(q * dest[here, :], 1, keepdims=True)
            low = neg_max[here, :]
            top = jnp.maximum(low, positive)
            pos_exp = jnp.exp(positive - top)
            shrink = jnp.exp(low - top)
            total = pos_exp + neg_sum[here, :] * shrink
            coef_pos = pos_exp / total - 1.0
            coef[here, :] = coef_pos
            grad_dest[here, :] = (coef_pos * q).astype(BF16)
            weights[here, :] = (neg_exp[here, :] * (shrink / total)).astype(BF16)

        make_grads(2)
        send_grads(2)

        @pl.loop(0, edges // (2 * CAP))
        def _(k):
            base = pl.multiple_of(k * 2 * CAP, 2 * CAP)
            here = pl.ds(base, 2 * CAP)
            grad_query = coef[here, :] * dest[here, :] + dot_nn(weights[here, :], table[...])
            grad_source = times_conjugate(
                grad_query, rel_edges[here, :].astype(F32), main, first, sign
            ).astype(BF16)
            spread = onehot(iota((rows, 2 * CAP), 0) == source_ids[pl.ds(s, 1), here])
            source_acc[...] += dot_nn(spread, grad_source)

        ar_fill(reduce, source_acc[...])
        ar_first(reduce)
        make_grads(0)
        send_grads(0)
        grad_recv[s, 0] = grad_send[s, 0]
        ar_scatter(reduce)
        make_grads(1)
        send_grads(1)
        make_grads(3)
        grads[...] = dot_tn(weights[...], query[...])
        ar_cross(reduce)
        send_grads(3)
        ar_gather(reduce)

        def scatter_grads(p):
            for k in (2 * p, 2 * p + 1):
                if k:
                    grad_copy(k).wait_send()
                    grad_arrival(k).wait_recv()
            arrived = [unpack(grad_recv[s, k].astype(F32), CAP, main, tail) for k in (2 * p, 2 * p + 1)]
            grads[...] += dot_nn(asked(p), jnp.concatenate(arrived, 0).astype(BF16))

        scatter_grads(2)
        scatter_grads(0)
        scatter_grads(1)
        ar_share(reduce)
        scatter_grads(3)
        ar_done(reduce)

        @pl.when(s == 0)
        def _():
            ids_wait(range(1, steps))

        total = grads[...] + jnp.where(m == root, ar_read(reduce), 0.0)
        fresh = state[...] + jnp.sum(total * total, 1, keepdims=True) * (1.0 / width)
        state[...] = fresh
        table[...] = (table[...].astype(F32) - total / jnp.sqrt(fresh)).astype(BF16)

    entity_out[...] = dot_nt(place[...], table[...]).astype(BF16)
    state_out[...] = jnp.sum(jnp.where(eye, state[...], 0.0), 0, keepdims=True)


def hand_over(table, state, table_out, state_out):
    table_out[...] = table[...]
    state_out[...] = state[...]


def per_device(
    groups,
    members,
    entity,
    adagrad_state,
    relation,
    source_ids,
    relation_ids,
    dest_groups,
    dest_rows,
    negative_ids,
    owners,
):
    rows, width = entity.shape
    steps, edges = source_ids.shape
    half = width // 2
    wide = 2 * (half // LANES * LANES) + LANES
    slots = groups * CAP
    depth = members // 4
    stack = CAP * width // LANES
    piece = -(-rows // 2 * width // LANES // depth // 8) * 8
    uses = 2 * steps
    dma = pltpu.SemaphoreType.DMA
    vmem = pltpu.VMEM
    whole = pl.BlockSpec(memory_space=pltpu.VMEM)
    table, state = pl.pallas_call(
        functools.partial(kernel, groups, members),
        out_shape=(
            jax.ShapeDtypeStruct((width, rows), BF16),
            jax.ShapeDtypeStruct((1, rows), F32),
        ),
        in_specs=[
            pl.BlockSpec(memory_space=pltpu.SMEM),
            whole,
            whole,
            pl.BlockSpec(memory_space=pl.ANY),
        ]
        + [whole] * 5,
        out_specs=(whole, whole),
        scratch_shapes=[
            vmem((width, wide), BF16),
            vmem((rows, wide), BF16),
            vmem((rows, 1), F32),
            vmem((width, relation.shape[0]), BF16),
            dma(()),
            vmem((relation.shape[0], wide), BF16),
            vmem((steps, edges, 1), jnp.int32),
            vmem((steps, edges, 1), jnp.int32),
            vmem((steps, 16, edges), BF16),
            vmem((steps, slots, edges), BF16),
            vmem((steps, edges, slots), BF16),
            vmem((steps, groups, 8, CAP), jnp.int32),
            vmem((steps, groups, 8, CAP), jnp.int32),
            vmem((8, rows), F32),
            vmem((edges, wide), BF16),
            vmem((edges, wide), BF16),
            vmem((edges, rows), F32),
            vmem((edges, 1), F32),
            vmem((edges, 1), F32),
            vmem((edges, rows), BF16),
            vmem((edges, 1), F32),
            vmem((edges, wide), F32),
            vmem((edges, wide), BF16),
            vmem((steps, groups, stack, LANES), BF16),
            vmem((steps, groups, stack, LANES), BF16),
            vmem((steps, groups, stack, LANES), BF16),
            vmem((steps, groups, stack, LANES), BF16),
            vmem((rows, wide), BF16),
            vmem((rows, wide), F32),
            vmem((rows, wide), F32),
            vmem((uses, 2, depth, piece, LANES), BF16),
            vmem((uses, depth, piece, LANES), BF16),
            vmem((uses, depth, piece, LANES), BF16),
            vmem((uses, depth, piece, LANES), BF16),
            vmem((uses, piece, LANES), BF16),
            vmem((uses, piece, LANES), BF16),
            vmem((uses, 2, depth, piece, LANES), BF16),
            dma((steps, groups)),
            dma((steps, groups)),
            dma((steps, groups)),
            dma((steps, groups)),
            dma((steps, groups)),
            dma((steps, groups)),
            dma((uses, depth)),
            dma((uses, depth)),
            dma((uses, depth)),
            dma((uses, depth)),
            dma((uses,)),
            dma((uses,)),
            dma((uses, depth)),
            dma((uses, depth)),
            dma((uses, depth)),
            dma((uses, depth)),
        ],
        compiler_params=pltpu.CompilerParams(
            collective_id=0, has_side_effects=True, vmem_limit_bytes=60 << 20
        ),
    )(
        owners,
        entity.T,
        adagrad_state.reshape(1, rows),
        relation.T,
        source_ids,
        relation_ids,
        jnp.transpose(dest_groups, (0, 2, 1)),
        dest_rows,
        negative_ids,
    )
    table, state = pl.pallas_call(
        hand_over,
        out_shape=(
            jax.ShapeDtypeStruct((width, rows), BF16),
            jax.ShapeDtypeStruct((1, rows), F32),
        ),
        in_specs=[whole, whole],
        out_specs=(whole, whole),
    )(table, state)
    return (table.T, state.reshape(rows))


def solution(mesh):
    placed = (
        P(("group", "member"), None),
        P(("group", "member")),
        P(),
        P(None, ("group", "member")),
        P(None, ("group", "member")),
        P(None, ("group", "member"), None),
        P(None, ("group", "member")),
        P(None, ("group", "member")),
        P(),
    )
    return jax.shard_map(
        functools.partial(per_device, mesh.shape["group"], mesh.shape["member"]),
        mesh=mesh,
        in_specs=placed,
        out_specs=(P(("group", "member"), None), P(("group", "member"))),
        check_vma=False,
    )
```

```python
import functools

import jax
import jax.numpy as jnp
from jax import lax
from jax.experimental import pallas as pl
from jax.experimental.pallas import tpu as pltpu
from jax.sharding import PartitionSpec as P

MESH = pl.DeviceIdType.MESH
F32 = jnp.float32
BF16 = jnp.bfloat16
LANES = 128
CAP = 128
LOW = -1e30


def dot_nn(a, b):
    return lax.dot_general(a, b, (((1,), (0,)), ((), ())), preferred_element_type=F32)


def dot_nt(a, b):
    return lax.dot_general(a, b, (((1,), (1,)), ((), ())), preferred_element_type=F32)


def dot_tn(a, b):
    return lax.dot_general(a, b, (((0,), (0,)), ((), ())), preferred_element_type=F32)


def iota(shape, dim):
    return lax.broadcasted_iota(jnp.int32, shape, dim)


def onehot(mask):
    return jnp.where(mask, 1.0, 0.0).astype(BF16)


def complex_parts(value, main):
    return value[:, :main], value[:, main : 2 * main], value[:, 2 * main :]


def tail_forms(tail, first):
    swapped = pltpu.roll(tail, LANES // 2, 1)
    return jnp.where(first, tail, swapped), jnp.where(first, swapped, tail)


def times(source, rel, main, first, sign):
    sr, si, st = complex_parts(source, main)
    rr, ri, rt = complex_parts(rel, main)
    tr, ti = tail_forms(rt, first)
    mixed = st * tr + sign * (pltpu.roll(st, LANES // 2, 1) * ti)
    return jnp.concatenate([sr * rr - si * ri, sr * ri + si * rr, mixed], 1)


def times_conjugate(grad, rel, main, first, sign):
    gr, gi, gt = complex_parts(grad, main)
    rr, ri, rt = complex_parts(rel, main)
    tr, ti = tail_forms(rt, first)
    mixed = gt * tr - sign * (pltpu.roll(gt, LANES // 2, 1) * ti)
    return jnp.concatenate([gr * rr + gi * ri, gi * rr - gr * ri, mixed], 1)


def pack(value, main, tail):
    count = value.shape[0]
    part = count // (LANES // 2 // tail)
    tiles = [value[:, c : c + LANES] for c in range(0, 2 * main, LANES)]
    last = value[:, 2 * main :]
    mixed = last[:part]
    for j in range(1, count // part):
        mixed = mixed + pltpu.roll(last[j * part : (j + 1) * part], tail * j, 1)
    return jnp.concatenate(tiles + [mixed], 0)


def unpack(stack, count, main, tail):
    part = count // (LANES // 2 // tail)
    tiles = 2 * main // LANES
    mixed = stack[tiles * count : tiles * count + part]
    used = iota((1, LANES), 1) % (LANES // 2) < tail
    last = [jnp.where(used, mixed, 0.0)]
    for j in range(1, count // part):
        last.append(jnp.where(used, pltpu.roll(mixed, LANES - tail * j, 1), 0.0))
    columns = [stack[c * count : (c + 1) * count] for c in range(tiles)]
    return jnp.concatenate(columns + [jnp.concatenate(last, 0)], 1)


def kernel(
    groups,
    members,
    owners,
    entity,
    state_in,
    relation,
    source_ids,
    relation_ids,
    dest_groups,
    dest_rows,
    negative_ids,
    entity_out,
    state_out,
    place,
    table,
    state,
    rel_raw,
    rel_sem,
    rel_table,
    edge_src,
    edge_rel,
    facts,
    taken,
    given,
    ids_send,
    ids_recv,
    counts,
    rel_edges,
    query,
    neg_exp,
    neg_max,
    neg_sum,
    weights,
    coef,
    dest,
    grad_dest,
    row_send,
    row_recv,
    grad_send,
    grad_recv,
    block,
    source_acc,
    grads,
    ar_in,
    ar_half,
    ar_mine,
    ar_parts,
    ar_piece,
    ar_other,
    ar_out,
    ids_ss,
    ids_rs,
    row_ss,
    row_rs,
    grad_ss,
    grad_rs,
    p1_ss,
    p1_rs,
    p2_ss,
    p2_rs,
    p3_ss,
    p3_rs,
    p4_ss,
    p4_rs,
    p5_ss,
    p5_rs,
):
    steps, edges = source_ids.shape
    width, rows = entity.shape
    rel_rows = relation.shape[1]
    half = width // 2
    main = half // LANES * LANES
    wide = table.shape[1]
    tail = half - main
    share = rows // 2
    piece = ar_half.shape[2]
    slots = groups * CAP
    depth = members // 4
    rings = groups // 2

    g = lax.axis_index("group")
    m = lax.axis_index("member")
    gx, gy = g // rings, g % rings
    core, z, xh = m % 2, (m // 2) % depth, m // (2 * depth)
    twin = m + 1 - 2 * core
    across = (m + 2 * depth) % members

    hops = [(0, j) for j in range(rings)]
    hops += sorted(((1, j) for j in range(rings)), key=lambda hop: -min(hop[1], rings - hop[1]))

    blocks = ((0, 1), (2, 3), (4, 6), (5, 7))

    def peer(k):
        return ((gx + hops[k][0]) % 2) * rings + (gy + hops[k][1]) % rings

    def mirror(k):
        return hops.index((hops[k][0], -hops[k][1] % rings))

    def floor(k):
        return (z + k) % depth

    def along(other):
        return (g, xh * (2 * depth) + other * 2 + core)

    def remote(src, dst, send_sem, recv_sem, device):
        return pltpu.make_async_remote_copy(
            src_ref=src,
            dst_ref=dst,
            send_sem=send_sem,
            recv_sem=recv_sem,
            device_id=device,
            device_id_type=MESH,
        )

    barrier = pltpu.get_barrier_semaphore()
    fetch_relation = pltpu.make_async_copy(relation, rel_raw, rel_sem)
    fetch_relation.start()

    for k in range(1, groups):
        pl.semaphore_signal(barrier, inc=1, device_id=(peer(k), m), device_id_type=MESH)
    for k in range(1, depth):
        pl.semaphore_signal(barrier, inc=1, device_id=along(floor(k)), device_id_type=MESH)
    pl.semaphore_signal(barrier, inc=1, device_id=(g, twin), device_id_type=MESH)
    pl.semaphore_signal(barrier, inc=1, device_id=(g, across), device_id_type=MESH)

    def ids_copy(s, k):
        return remote(
            ids_send.at[s, k],
            ids_recv.at[s, mirror(k)],
            ids_ss.at[s, k],
            ids_rs.at[s, mirror(k)],
            (peer(k), m),
        )

    def ids_arrival(s, k):
        return remote(
            ids_send.at[s, k], ids_recv.at[s, k], ids_ss.at[s, k], ids_rs.at[s, k], (peer(k), m)
        )

    def assign_slots(turns):
        before = onehot(iota((edges, edges), 0) < iota((edges, edges), 1))
        for s in turns:
            group_row = dest_groups[s]
            hop_x = (group_row // rings + 2 - gx) % 2
            hop_y = (group_row % rings + rings - gy) % rings
            where = hop_x * rings + hop_y
            hop = jnp.zeros_like(where)
            for k in range(groups):
                hop = jnp.where(where == hops[k][0] * rings + hops[k][1], k, hop)
            named = iota((16, edges), 0) == hop
            rank = dot_nn(onehot(named), before)
            rank = jnp.sum(jnp.where(named, rank, 0.0), 0, keepdims=True).astype(jnp.int32)
            taken[s] = onehot(iota((slots, edges), 0) == hop * CAP + rank)
            rel_row = relation_ids[s : s + 1, :]
            high = rel_row // 32
            which = iota((16, edges), 0)
            known = jnp.where(which == 0, source_ids[s : s + 1, :], 0)
            known = jnp.where(which == 1, high, known)
            known = jnp.where(which == 2, rel_row - 32 * high, known)
            known = jnp.where(which == 3, dest_rows[s : s + 1, :], known)
            known = jnp.where(which == 4, 1, known)
            known = jnp.where(which == 5, hop, known)
            known = jnp.where(which == 6, rank, known)
            facts[s] = known.astype(F32).astype(BF16)
            flat = dot_nt(facts[s], taken[s]).astype(jnp.int32)
            wanted = flat[3:4, :] + 4 * rows * (flat[4:5, :] - 1)
            for k in range(groups):
                ids_send[s, k] = jnp.broadcast_to(wanted[:, k * CAP : (k + 1) * CAP], (8, CAP))

    def ids_start(turns):
        for s in turns:
            for k in range(1, groups):
                ids_copy(s, k).start()
            ids_recv[s, 0] = ids_send[s, 0]

    assign_slots(range(1))
    pl.semaphore_wait(barrier, groups + depth)
    ids_start(range(1))

    comp = iota((width, 1), 0)
    imag = comp >= half
    local = jnp.where(imag, comp - half, comp)
    spot = jnp.where(
        local < main,
        local + jnp.where(imag, main, 0),
        2 * main + jnp.where(imag, LANES // 2, 0) + local - main,
    )
    place[...] = onehot(iota((width, wide), 1) == spot)
    table[...] = dot_tn(entity[...], place[...]).astype(BF16)
    eye = iota((rows, rows), 0) == iota((rows, rows), 1)
    state[...] = jnp.sum(jnp.where(eye, state_in[...], 0.0), 1, keepdims=True)
    first = iota((1, LANES), 1) < LANES // 2
    sign = jnp.where(first, -1.0, 1.0)

    def edge_columns():
        same = onehot(iota((edges, edges), 0) == iota((edges, edges), 1))
        for s in range(steps):
            tall = dot_nt(same, facts[s]).astype(jnp.int32)
            edge_src[s] = tall[:, 0:1]
            edge_rel[s] = 32 * tall[:, 1:2] + tall[:, 2:3]
            given[s] = onehot(iota((edges, slots), 1) == CAP * tall[:, 5:6] + tall[:, 6:7])

    def ids_wait(turns):
        for s in turns:
            for k in range(1, groups):
                ids_copy(s, k).wait_send()
                ids_arrival(s, k).wait_recv()

    near = sorted(range(1, depth), key=lambda k: min(k, depth - k))
    far = near[::-1]

    def ar_fill(i, value):
        for h in range(2):
            stack = pack(value[h * share : (h + 1) * share], main, tail)
            spare = jnp.zeros((depth * piece - stack.shape[0], LANES), F32)
            stack = jnp.concatenate([stack, spare], 0)
            ar_in[i, h] = stack.reshape(depth, piece, LANES).astype(BF16)

    def ar_read(i):
        halves = []
        for h in range(2):
            stack = ar_out[i, h].astype(F32).reshape(depth * piece, LANES)
            halves.append(unpack(stack, share, main, tail))
        return jnp.concatenate(halves, 0)

    def ar_first_copy(i, other):
        return remote(
            ar_in.at[i, 1 - core, other],
            ar_half.at[i, other],
            p1_ss.at[i, other],
            p1_rs.at[i, other],
            (g, twin),
        )

    def ar_first(i):
        for k in far + [0]:
            ar_first_copy(i, floor(k)).start()

    def ar_scatter_copy(i, other):
        return remote(
            ar_mine.at[i, other],
            ar_parts.at[i, z],
            p2_ss.at[i, other],
            p2_rs.at[i, z],
            along(other),
        )

    def ar_scatter_arrival(i, other):
        return remote(
            ar_mine.at[i, other],
            ar_parts.at[i, other],
            p2_ss.at[i, other],
            p2_rs.at[i, other],
            along(other),
        )

    def ar_cross_copy(i):
        return remote(ar_piece.at[i], ar_other.at[i], p3_ss.at[i], p3_rs.at[i], (g, across))

    def ar_gather_copy(i, other):
        return remote(
            ar_out.at[i, core, z],
            ar_out.at[i, core, z],
            p4_ss.at[i, other],
            p4_rs.at[i, z],
            along(other),
        )

    def ar_gather_arrival(i, other):
        return remote(
            ar_out.at[i, core, other],
            ar_out.at[i, core, other],
            p4_ss.at[i, other],
            p4_rs.at[i, other],
            along(other),
        )

    def ar_last(i, which, other):
        return remote(
            ar_out.at[i, which, other],
            ar_out.at[i, which, other],
            p5_ss.at[i, other],
            p5_rs.at[i, other],
            (g, twin),
        )

    def ar_scatter(i):
        for k in far + [0]:
            other = floor(k)
            ar_first_copy(i, other).wait()
            mine = ar_in[i, core, other].astype(F32) + ar_half[i, other].astype(F32)
            ar_mine[i, other] = mine.astype(BF16)
            if k:
                ar_scatter_copy(i, other).start()

    def ar_cross(i):
        @pl.loop(1, depth)
        def _(k):
            other = floor(k)
            ar_scatter_copy(i, other).wait_send()
            ar_scatter_arrival(i, other).wait_recv()

        ar_parts[i, z] = ar_mine[i, z]
        piece = jnp.sum(ar_parts[i].astype(F32), 0)
        ar_piece[i] = piece.astype(BF16)
        ar_cross_copy(i).start()

    def ar_gather(i):
        ar_cross_copy(i).wait()
        whole = ar_piece[i].astype(F32) + ar_other[i].astype(F32)
        ar_out[i, core, z] = whole.astype(BF16)
        for k in far:
            ar_gather_copy(i, floor(k)).start()
        ar_last(i, core, z).start()

    def ar_share(i):
        for k in near:
            other = floor(k)
            ar_gather_arrival(i, other).wait_recv()
            ar_last(i, core, other).start()

    def ar_done(i):
        for k in [0] + near:
            other = floor(k)
            if k:
                ar_gather_copy(i, other).wait_send()
            ar_last(i, core, other).wait_send()
            ar_last(i, 1 - core, other).wait_recv()

    @pl.loop(0, steps)
    def _(s):
        root = owners[s, g]
        fetch, reduce = 2 * s, 2 * s + 1

        def row_copy(k):
            return remote(
                row_send.at[s, k],
                row_recv.at[s, mirror(k)],
                row_ss.at[s, k],
                row_rs.at[s, mirror(k)],
                (peer(k), m),
            )

        def row_arrival(k):
            return remote(
                row_send.at[s, k], row_recv.at[s, k], row_ss.at[s, k], row_rs.at[s, k], (peer(k), m)
            )

        def grad_copy(k):
            return remote(
                grad_send.at[s, k],
                grad_recv.at[s, mirror(k)],
                grad_ss.at[s, k],
                grad_rs.at[s, mirror(k)],
                (peer(k), m),
            )

        def grad_arrival(k):
            return remote(
                grad_send.at[s, k],
                grad_recv.at[s, k],
                grad_ss.at[s, k],
                grad_rs.at[s, k],
                (peer(k), m),
            )

        def asked(ks):
            ids = [ids_recv[s, k, 0:1, :] for k in ks]
            return onehot(iota((rows, 2 * CAP), 0) == jnp.concatenate(ids, 1))

        def pick_rows(p):
            picked = dot_tn(asked((2 * p, 2 * p + 1)), table[...])
            for j in range(2):
                row_send[s, 2 * p + j] = pack(picked[j * CAP : (j + 1) * CAP], main, tail).astype(BF16)

        def send_rows(p):
            for k in (2 * p, 2 * p + 1):
                if k:
                    row_copy(k).start()

        def relations(k):
            here = pl.ds(pl.multiple_of(k * 2 * CAP, 2 * CAP), 2 * CAP)
            chosen = onehot(iota((2 * CAP, rel_rows), 1) == edge_rel[s, here, :])
            rel_edges[here, :] = dot_nn(chosen, rel_table[...]).astype(BF16)

        def collect(ks):
            for k in ks:
                if k:
                    row_copy(k).wait_send()
                    row_arrival(k).wait_recv()
            arrived = [unpack(row_recv[s, k].astype(F32), CAP, main, tail) for k in ks]
            arrived = jnp.concatenate(arrived, 0).astype(BF16)
            into = jnp.concatenate([given[s, :, k * CAP : (k + 1) * CAP] for k in ks], 1)
            sorted_rows = dot_nn(into, arrived)
            dest[...] = dest[...] + sorted_rows if ks[0] else sorted_rows

        def make_grads(p):
            block_rows = taken[s, 2 * p * CAP : (2 * p + 2) * CAP, :]
            spread = dot_nn(block_rows, grad_dest[...])
            for j in range(2):
                stack = pack(spread[j * CAP : (j + 1) * CAP], main, tail)
                grad_send[s, 2 * p + j] = stack.astype(BF16)

        def send_grads(p):
            for k in (2 * p, 2 * p + 1):
                if k:
                    grad_copy(k).start()

        @pl.when(s > 0)
        def _():
            pick_rows(2)
            send_rows(2)

        ar_fill(fetch, jnp.where(m == root, table[...].astype(F32), 0.0))
        ar_first(fetch)
        ar_scatter(fetch)

        @pl.when(s == 0)
        def _():
            ids_wait(range(1))
            pick_rows(2)
            row_copy(4).start()

        pick_rows(0)
        send_rows(0)
        row_recv[s, 0] = row_send[s, 0]
        pick_rows(1)
        send_rows(1)
        pick_rows(3)

        @pl.when(s == 0)
        def _():
            assign_slots(range(1, steps))
            ids_start(range(1, steps))
            edge_columns()
            fetch_relation.wait()
            rel_table[...] = dot_tn(rel_raw[...], place[...]).astype(BF16)

        slot_count = negative_ids.shape[1]
        hits = onehot(iota((rows, slot_count), 0) == negative_ids[pl.ds(s, 1), :])
        counts[...] = dot_nt(jnp.ones((8, slot_count), BF16), hits)
        ar_cross(fetch)

        @pl.when(s == 0)
        def _():
            row_copy(5).start()

        send_rows(3)

        relations(0)
        ar_gather(fetch)
        relations(1)
        ar_share(fetch)
        source_acc[...] = jnp.zeros_like(source_acc)
        count_row = counts[0:1, :]
        present = count_row > 0.5
        ar_done(fetch)
        block[...] = ar_read(fetch).astype(BF16)

        @pl.loop(0, edges // (2 * CAP))
        def _(k):
            here = pl.ds(pl.multiple_of(k * 2 * CAP, 2 * CAP), 2 * CAP)
            chosen = onehot(iota((2 * CAP, rows), 1) == edge_src[s, here, :])
            source = dot_nn(chosen, block[...])
            q = times(source, rel_edges[here, :].astype(F32), main, first, sign).astype(BF16)
            query[here, :] = q
            scores = jnp.where(present, dot_nt(q, table[...]), LOW)
            top = jnp.max(scores, 1, keepdims=True)
            e = jnp.exp(scores - top) * count_row
            neg_exp[here, :] = e
            neg_max[here, :] = top
            neg_sum[here, :] = jnp.sum(e, 1, keepdims=True)

        for ks in blocks:
            collect(ks)

        @pl.loop(0, edges // (2 * CAP))
        def _(k):
            here = pl.ds(pl.multiple_of(k * 2 * CAP, 2 * CAP), 2 * CAP)
            q = query[here, :].astype(F32)
            positive = jnp.sum(q * dest[here, :], 1, keepdims=True)
            low = neg_max[here, :]
            top = jnp.maximum(low, positive)
            pos_exp = jnp.exp(positive - top)
            shrink = jnp.exp(low - top)
            total = pos_exp + neg_sum[here, :] * shrink
            coef_pos = pos_exp / total - 1.0
            coef[here, :] = coef_pos
            grad_dest[here, :] = (coef_pos * q).astype(BF16)
            weights[here, :] = (neg_exp[here, :] * (shrink / total)).astype(BF16)

        make_grads(2)
        send_grads(2)

        @pl.loop(0, edges // (2 * CAP))
        def _(k):
            base = pl.multiple_of(k * 2 * CAP, 2 * CAP)
            here = pl.ds(base, 2 * CAP)
            grad_query = coef[here, :] * dest[here, :] + dot_nn(weights[here, :], table[...])
            grad_source = times_conjugate(
                grad_query, rel_edges[here, :].astype(F32), main, first, sign
            ).astype(BF16)
            spread = onehot(iota((rows, 2 * CAP), 0) == source_ids[pl.ds(s, 1), here])
            source_acc[...] += dot_nn(spread, grad_source)

        ar_fill(reduce, source_acc[...])
        ar_first(reduce)
        make_grads(0)
        send_grads(0)
        grad_recv[s, 0] = grad_send[s, 0]
        ar_scatter(reduce)
        make_grads(1)
        send_grads(1)
        make_grads(3)
        grads[...] = dot_tn(weights[...], query[...])
        ar_cross(reduce)
        send_grads(3)
        ar_gather(reduce)

        def scatter_grads(ks):
            for k in ks:
                if k:
                    grad_copy(k).wait_send()
                    grad_arrival(k).wait_recv()
            arrived = [unpack(grad_recv[s, k].astype(F32), CAP, main, tail) for k in ks]
            grads[...] += dot_nn(asked(ks), jnp.concatenate(arrived, 0).astype(BF16))

        for ks in blocks[:2]:
            scatter_grads(ks)
        ar_share(reduce)
        for ks in blocks[2:]:
            scatter_grads(ks)
        ar_done(reduce)

        @pl.when(s == 0)
        def _():
            ids_wait(range(1, steps))

        total = grads[...] + jnp.where(m == root, ar_read(reduce), 0.0)
        fresh = state[...] + jnp.sum(total * total, 1, keepdims=True) * (1.0 / width)
        state[...] = fresh
        table[...] = (table[...].astype(F32) - total / jnp.sqrt(fresh)).astype(BF16)

    entity_out[...] = dot_nt(place[...], table[...]).astype(BF16)
    state_out[...] = jnp.sum(jnp.where(eye, state[...], 0.0), 0, keepdims=True)


def hand_over(table, state, table_out, state_out):
    table_out[...] = table[...]
    state_out[...] = state[...]


def per_device(
    groups,
    members,
    entity,
    adagrad_state,
    relation,
    source_ids,
    relation_ids,
    dest_groups,
    dest_rows,
    negative_ids,
    owners,
):
    rows, width = entity.shape
    steps, edges = source_ids.shape
    half = width // 2
    wide = 2 * (half // LANES * LANES) + LANES
    slots = groups * CAP
    depth = members // 4
    stack = CAP * width // LANES
    piece = -(-rows // 2 * width // LANES // depth // 8) * 8
    uses = 2 * steps
    dma = pltpu.SemaphoreType.DMA
    vmem = pltpu.VMEM
    whole = pl.BlockSpec(memory_space=pltpu.VMEM)
    table, state = pl.pallas_call(
        functools.partial(kernel, groups, members),
        out_shape=(
            jax.ShapeDtypeStruct((width, rows), BF16),
            jax.ShapeDtypeStruct((1, rows), F32),
        ),
        in_specs=[
            pl.BlockSpec(memory_space=pltpu.SMEM),
            whole,
            whole,
            pl.BlockSpec(memory_space=pl.ANY),
        ]
        + [whole] * 5,
        out_specs=(whole, whole),
        scratch_shapes=[
            vmem((width, wide), BF16),
            vmem((rows, wide), BF16),
            vmem((rows, 1), F32),
            vmem((width, relation.shape[0]), BF16),
            dma(()),
            vmem((relation.shape[0], wide), BF16),
            vmem((steps, edges, 1), jnp.int32),
            vmem((steps, edges, 1), jnp.int32),
            vmem((steps, 16, edges), BF16),
            vmem((steps, slots, edges), BF16),
            vmem((steps, edges, slots), BF16),
            vmem((steps, groups, 8, CAP), jnp.int32),
            vmem((steps, groups, 8, CAP), jnp.int32),
            vmem((8, rows), F32),
            vmem((edges, wide), BF16),
            vmem((edges, wide), BF16),
            vmem((edges, rows), F32),
            vmem((edges, 1), F32),
            vmem((edges, 1), F32),
            vmem((edges, rows), BF16),
            vmem((edges, 1), F32),
            vmem((edges, wide), F32),
            vmem((edges, wide), BF16),
            vmem((steps, groups, stack, LANES), BF16),
            vmem((steps, groups, stack, LANES), BF16),
            vmem((steps, groups, stack, LANES), BF16),
            vmem((steps, groups, stack, LANES), BF16),
            vmem((rows, wide), BF16),
            vmem((rows, wide), F32),
            vmem((rows, wide), F32),
            vmem((uses, 2, depth, piece, LANES), BF16),
            vmem((uses, depth, piece, LANES), BF16),
            vmem((uses, depth, piece, LANES), BF16),
            vmem((uses, depth, piece, LANES), BF16),
            vmem((uses, piece, LANES), BF16),
            vmem((uses, piece, LANES), BF16),
            vmem((uses, 2, depth, piece, LANES), BF16),
            dma((steps, groups)),
            dma((steps, groups)),
            dma((steps, groups)),
            dma((steps, groups)),
            dma((steps, groups)),
            dma((steps, groups)),
            dma((uses, depth)),
            dma((uses, depth)),
            dma((uses, depth)),
            dma((uses, depth)),
            dma((uses,)),
            dma((uses,)),
            dma((uses, depth)),
            dma((uses, depth)),
            dma((uses, depth)),
            dma((uses, depth)),
        ],
        compiler_params=pltpu.CompilerParams(
            collective_id=0, has_side_effects=True, vmem_limit_bytes=60 << 20
        ),
    )(
        owners,
        entity.T,
        adagrad_state.reshape(1, rows),
        relation.T,
        source_ids,
        relation_ids,
        jnp.transpose(dest_groups, (0, 2, 1)),
        dest_rows,
        negative_ids,
    )
    table, state = pl.pallas_call(
        hand_over,
        out_shape=(
            jax.ShapeDtypeStruct((width, rows), BF16),
            jax.ShapeDtypeStruct((1, rows), F32),
        ),
        in_specs=[whole, whole],
        out_specs=(whole, whole),
    )(table, state)
    return (table.T, state.reshape(rows))


def solution(mesh):
    placed = (
        P(("group", "member"), None),
        P(("group", "member")),
        P(),
        P(None, ("group", "member")),
        P(None, ("group", "member")),
        P(None, ("group", "member"), None),
        P(None, ("group", "member")),
        P(None, ("group", "member")),
        P(),
    )
    return jax.shard_map(
        functools.partial(per_device, mesh.shape["group"], mesh.shape["member"]),
        mesh=mesh,
        in_specs=placed,
        out_specs=(P(("group", "member"), None), P(("group", "member"))),
        check_vma=False,
    )
```
